32 devices in a mesh: tm: 4 (over x, core), rows: 8 (over z, y).
Axes of the slice: x: 2, y: 2, z: 4, core: 2. Of those that a mesh axis runs over, the one named last changes fastest.
Arguments:
- smoother_gains: bfloat16 [4, 1536, 1536], P('tm', 'rows'), may hold values from -1 to 1
- smoother_offsets: bfloat16 [4, 1536], P('tm', 'rows'), may hold values from -6 to 6
- smoother_covs: bfloat16 [4, 1536, 1536], P('tm', 'rows'), may hold values from -1 to 4, as said below
Outputs:
- smoothed_means: bfloat16 [4, 1536], P('tm', 'rows')
- smoothed_covs: bfloat16 [4, 1536, 1536], P('tm', 'rows')
The draws below stay inside these ranges and needn't reach their ends.
Inputs may be any that keep to these rules, and one draw needn't show every extreme that they name: `smoother_covs`: each step's covariance matrix is symmetric.
All inputs are finite; a program needn't handle non-finite values.
Results may differ from the reference program's by a relative error of at most 0.025.
Values may be sent and summed in bfloat16 or wider, within the bound.
A program may use at most 64 MiB of HBM per device.

```python
import math
import jax
import jax.numpy as jnp
from jax import lax

NS = 1536
STEPS = 4


def draw_smoother_gains(key, part):
    first_key, second_key = jax.random.split(jax.random.fold_in(key, 11))
    rate_diag = jax.random.uniform(first_key, (STEPS, NS), jnp.float32, 0.3, 0.95)
    noise_part = jax.random.normal(second_key, (STEPS, NS, NS), jnp.float32) * (0.3 / math.sqrt(NS))
    identity_mat = jnp.eye(NS, dtype=jnp.float32)
    combined = noise_part + identity_mat[None, :, :] * rate_diag[:, :, None]
    return jnp.clip(combined, -1.0, 1.0).astype(jnp.bfloat16)


def draw_smoother_covs(key, part):
    first_key, second_key = jax.random.split(jax.random.fold_in(key, 23))
    scale_diag = jnp.exp(jax.random.uniform(first_key, (STEPS, NS), jnp.float32, math.log(0.5), math.log(2.0)))
    noise_part = jax.random.normal(second_key, (STEPS, NS, NS), jnp.float32) * (0.1 / math.sqrt(NS))
    noise_part = jnp.clip(noise_part, -0.5, 0.5)
    symmetric = noise_part + jnp.swapaxes(noise_part, 1, 2)
    identity_mat = jnp.eye(NS, dtype=jnp.float32)
    return (symmetric + identity_mat[None, :, :] * scale_diag[:, :, None]).astype(jnp.bfloat16)


def block_levels(rng, dims, shards, low, high):
    level = 1.0
    for position, shards_of in shards:
        heights = jax.random.uniform(jax.random.fold_in(jax.random.fold_in(rng, 6), position), (shards_of,), jnp.float32, low / len(shards), high / len(shards))
        level = level * jnp.repeat(jnp.exp(heights), dims[position] // shards_of).reshape((-1,) + (1,) * (len(dims) - 1 - position))
    return level


def noise(own_key, dims, width, most, cuts=(), held_as=jnp.bfloat16):
    array = jax.random.normal(own_key, dims, jnp.float32) * width
    if len(cuts) > 0:
        array = block_levels(own_key, dims, cuts, -0.22, 0.18) * array
    return jnp.clip(array, min=-most, max=most).astype(held_as)


def setup_inputs(seed: int = 0) -> dict:
    key_list = jax.random.split(jax.random.key(seed), 4)
    smoother_gains = draw_smoother_gains(jax.random.fold_in(key_list[3], 71), 0)
    smoother_offsets = noise(key_list[1], (STEPS, NS), 1.0, 6.0, ((0, 4), (1, 8)))
    smoother_covs = draw_smoother_covs(jax.random.fold_in(key_list[3], 71), 0)
    return dict(smoother_gains=smoother_gains, smoother_offsets=smoother_offsets, smoother_covs=smoother_covs)


def reference(smoother_gains, smoother_offsets, smoother_covs):
    mean_now = smoother_offsets[STEPS - 1]
    cov_now = smoother_covs[STEPS - 1]
    mean_list = [mean_now]
    cov_list = [cov_now]
    for step_back in range(STEPS - 2, -1, -1):
        left_gain = smoother_gains[step_back]
        mean_sum = jnp.dot(left_gain, mean_now, preferred_element_type=jnp.float32)
        mean_now = (mean_sum + smoother_offsets[step_back].astype(jnp.float32)).astype(jnp.bfloat16)
        left_times = jnp.dot(left_gain, cov_now, preferred_element_type=jnp.float32).astype(jnp.bfloat16)
        product_full = lax.dot_general(left_times, left_gain, (((1,), (1,)), ((), ())), preferred_element_type=jnp.float32)
        cov_now = (product_full + smoother_covs[step_back].astype(jnp.float32)).astype(jnp.bfloat16)
        mean_list.append(mean_now)
        cov_list.append(cov_now)
    return (jnp.stack(mean_list[::-1]), jnp.stack(cov_list[::-1]))
```

```python
import functools
import math

import jax
import jax.numpy as jnp
from jax import lax
from jax.experimental import pallas as pl
from jax.experimental.pallas import tpu as pltpu
from jax.sharding import PartitionSpec as P

MESH = pl.DeviceIdType.MESH
LANES = 128
PAD = 16
CHUNK = 32
LAG = 3
GREET = 4
LEFT_PARTS = 2
TILES_AT_ONCE = 2
CONTRACT_LAST = (((1,), (1,)), ((), ()))


def ring_row(place, n):
    side = place // (n // 2)
    return (1 - side) * 2 * place + side * (2 * (n - 1 - place) + 1)


def ring_place(row, n):
    odd = row % 2
    return (1 - odd) * (row // 2) + odd * (n - 1 - row // 2)


def unit_rows(rows):
    return math.gcd(rows, LANES)


def folded(rows):
    unit = unit_rows(rows)
    return (unit + unit // 2, LANES) if rows == 192 else (unit, rows)


def kernel(
    steps, n, gain_in, offset_in, cov_hbm, out,
    e_half, stage, cov, l_in, left_out, left_in, left, gbuf, gsum,
    e2_send, e2_recv, ring_send, ring_recv, pass_send, full_recv, init_send, stage_sems,
    l_send, l_recv, top_sems, load_sems, g_send, g_recv, gb_send, gb_recv,
    left_send, left_recv, fwd_send, x_send, x_recv, out_send, out_recv, mid_sems,
    low_send, low_recv,
):
    t = lax.axis_index("tm")
    r = lax.axis_index("rows")
    place = ring_place(r, n)
    right = ring_row((place + 1) % n, n)
    back = ring_row((place + n - 1) % n, n)
    quads = steps // 4
    gathers = e_half.shape[0]
    q = t // 4
    b = q * 4
    j_own = t % 4
    p = j_own // 2
    core = t % 2
    top = q == quads - 1
    partner = b + 2 * (1 - p) + 1
    size = gain_in.shape[1]
    rows = size // n
    half = size // 2
    unit = unit_rows(rows)
    per = rows // unit
    upt = LANES // unit
    tiles = half // LANES
    units = half // unit
    chunks = unit // CHUNK

    def aligned(x, m):
        return pl.multiple_of(x, m)

    def remote(src, dst, send, recv, device):
        return pltpu.make_async_remote_copy(
            src_ref=src, dst_ref=dst, send_sem=send, recv_sem=recv,
            device_id=device, device_id_type=MESH,
        )

    def plane_of(d, i):
        return ((per * d + i) // upt) % 2

    def place_of(d, i):
        u = per * d + i
        return (u // upt // 2) * upt + u % upt

    def way_of(d, i):
        return (per * d + i) % 2

    def owner(v):
        u = ((v // upt) * 2 + p) * upt + v % upt
        return u // per, u % per

    def unit_span(v, c, length):
        return pl.ds(aligned(v * unit + c * CHUNK, CHUNK), length)

    def nat_columns(tile, plane):
        return pl.ds(aligned((tile * 2 + plane) * LANES, LANES), LANES)

    def half_columns(tile):
        return pl.ds(aligned(tile * LANES, LANES), LANES)

    def other_row(i):
        return ring_row((place + i) % n, n)

    barrier = pltpu.get_barrier_semaphore()

    def greet(tt, rr):
        pl.semaphore_signal(barrier, inc=1, device_id=(tt, rr), device_id_type=MESH)

    for i in range(1, 4):
        greet(b + (j_own + i) % 4, r)
    for i in range(4):
        for rr in (right, back):
            greet(b + i, rr)

    @pl.when(core == 1)
    def _():
        def greet_row(i, carry):
            greet(t, other_row(i))
            return carry

        lax.fori_loop(2, n - 1, greet_row, 0)

    greetings = 3 + 8 + core * (n - 3)
    if quads > 1:
        for step in (-4, 4):
            near = (q * 4 + step >= 0) & (q * 4 + step < steps)

            @pl.when((core == 1) & near)
            def _():
                for i in (1, 3):
                    greet(b + step + i, r)

        greetings = greetings + core * 2 * (((q + quads - 1) // quads) + (2 * quads - 2 - q) // quads * 1)

    @pl.when(j_own == 3)
    def _():
        pltpu.make_async_copy(cov_hbm, cov.at[3, pl.ds(0, rows), :], load_sems.at[0]).start()

    pl.semaphore_wait(barrier, greetings)

    def init_copies(j, slot, src, recv, first_core):
        copies = []
        for i in range(per):
            x, v, w = plane_of(r, i), place_of(r, i), way_of(r, i)
            neighbour = right * (1 - w) + back * w
            for c in range(chunks):
                copies.append(remote(
                    src.at[pl.ds(i * unit + c * CHUNK, CHUNK), :],
                    e_half.at[j, unit_span(v, c, CHUNK), :],
                    init_send.at[slot, i, c], recv(i, c),
                    (b + 2 * x + first_core, neighbour),
                ))
        return copies

    def own_copies(j, slot, src, recv):
        copies = []
        for i in range(per):
            x, v = plane_of(r, i), place_of(r, i)
            copies.append(remote(
                src.at[pl.ds(i * unit, unit), :],
                e_half.at[j, unit_span(v, 0, unit), :],
                init_send.at[slot, i, chunks], recv(i),
                (b + 2 * x + 1, r),
            ))
        return copies

    def e2_init():
        return init_copies(2, 0, gain_in, lambda i, c: e2_recv.at[r, i, c], 1)

    def e2_own():
        return own_copies(2, 0, gain_in, lambda i: e2_recv.at[r, i, 0])

    def ring_init(j, slot):
        src = gain_in if j == 0 else stage
        return init_copies(j, slot, src, lambda i, c: ring_recv.at[j, r, i, c], 0)

    def ring_own(j, slot):
        src = gain_in if j == 0 else stage
        return own_copies(j, slot, src, lambda i: full_recv.at[j])

    def stage_copy():
        return remote(gain_in, stage, stage_sems.at[0], stage_sems.at[1], (t - 1, r))

    def whole_arrival(j):
        return remote(e_half.at[j], e_half.at[j], stage_sems.at[0], full_recv.at[j], (t - 1, r))

    def l_copy(j, plane, tile):
        return remote(
            cov_hbm.at[:, nat_columns(tile, plane)],
            l_in.at[j, :, half_columns(tile)],
            l_send.at[plane, tile], l_recv.at[j, tile], (b + 2 * plane + 1, r),
        )

    def l_local(j, tile):
        return pltpu.make_async_copy(
            cov_hbm.at[:, nat_columns(tile, p)], l_in.at[j, :, half_columns(tile)],
            l_recv.at[j, tile],
        )

    def top_copy():
        return remote(
            cov_hbm, cov.at[3, pl.ds(0, rows), :], top_sems.at[0], top_sems.at[1], (t - 2 * (2 * p - 1), r)
        )

    def g_copy(plane):
        return remote(
            offset_in, gbuf.at[r, j_own], g_send.at[plane], g_recv.at[j_own], (b + 2 * plane + 1, r)
        )

    def g_bundle(o, source):
        return remote(gbuf.at[source], gbuf.at[source], gb_send.at[o], gb_recv.at[source], (t, o))

    def left_copy(j, d, i, v):
        return remote(
            left_out.at[j, v], left_in.at[j, r, i], left_send.at[j, v], left_recv.at[j, r, i], (t, d)
        )

    def left_across(j, v, i):
        return remote(
            left_out.at[j, v], left_in.at[j, r, i], fwd_send.at[j, r, i], left_recv.at[j, r, i],
            (partner, r),
        )

    def left_pass(j, o, i):
        return remote(
            left_in.at[j, o, i], left_in.at[j, o, i], fwd_send.at[j, o, i], left_recv.at[j, o, i],
            (partner, r),
        )

    def x_copy(j, tile, plane):
        columns = nat_columns(tile, plane)
        return remote(
            cov.at[j, :, columns], cov.at[j, :, columns], x_send.at[j, tile], x_recv.at[j, tile],
            (partner, r),
        )

    def out_copy(tile, plane):
        columns = nat_columns(tile, plane)
        return remote(
            cov.at[0, :, columns], out.at[:, columns], out_send.at[tile],
            out_recv.at[tile * 2 + plane], (b, r),
        )

    def mid_copy():
        return remote(cov.at[2], out, mid_sems.at[0], mid_sems.at[1], (b + 2, r))

    def low_copy(tile, plane, dest):
        columns = nat_columns(tile, plane)
        return remote(
            cov.at[0, :, columns], cov.at[gathers, :, columns], low_send.at[dest, tile],
            low_recv.at[tile * 2 + plane], (b - 4 + 2 * dest + 1, r),
        )

    def both(copies, what):
        for copy in copies:
            getattr(copy, what)()

    def send_l(j):
        for plane in range(2):
            for tile in range(tiles):
                @pl.when(b + 2 * plane + 1 != t)
                def _():
                    l_copy(j, plane, tile).start()

                @pl.when(b + 2 * plane + 1 == t)
                def _():
                    l_local(j, tile).start()

    def l_gone(j):
        for plane in range(2):
            for tile in range(tiles):
                @pl.when(b + 2 * plane + 1 != t)
                def _():
                    l_copy(j, plane, tile).wait_send()

    def send_g():
        for plane in range(2):
            @pl.when(b + 2 * plane + 1 != t)
            def _():
                g_copy(plane).start()

    def g_gone():
        for plane in range(2):
            @pl.when(b + 2 * plane + 1 != t)
            def _():
                g_copy(plane).wait_send()

    def hop_units(hop, act):
        for i in range(per):
            for w in range(2):
                o = other_row(n - hop if w == 0 else hop)

                @pl.when((plane_of(o, i) == p) & (way_of(o, i) == w))
                def _():
                    act(o, i, right if w == 0 else back)

    @pl.when(core == 0)
    def _mover():
        @pl.when(j_own == 2)
        def _():
            both(e2_init(), "start")
            both(e2_own(), "start")
            send_g()
            send_l(2)

        @pl.when(j_own == 0)
        def _():
            send_g()
            stage_copy().wait_recv()
            both(ring_init(1, 1), "start")
            both(ring_own(1, 1), "start")
            send_l(0)

        def ring_copy(j, o, i, c, to):
            span = unit_span(place_of(o, i), c, CHUNK)
            return remote(
                e_half.at[j, span, :], e_half.at[j, span, :],
                ring_send.at[j, o, i, c], ring_recv.at[j, o, i, c], (t, to),
            )

        def pass_copy(j, o, i, c):
            span = unit_span(place_of(o, i), c, CHUNK)
            return remote(
                e_half.at[j, span, :], e_half.at[j, span, :],
                pass_send.at[j, o, i, c], full_recv.at[j], (t + 1, r),
            )

        def ring(j):
            def hop_step(hop, carry):
                def act(o, i, to):
                    for c in range(chunks):
                        ring_copy(j, o, i, c, to).wait_recv()

                        @pl.when(hop < n - 1)
                        def _():
                            ring_copy(j, o, i, c, to).start()

                        pass_copy(j, o, i, c).start()

                hop_units(hop, act)
                if j == 1:
                    @pl.when((hop == GREET) & (j_own == 0))
                    def _():
                        both(ring_init(0, 0), "start")
                return carry

            lax.fori_loop(1, n, hop_step, 0)

        if quads > 1:
            @pl.when(q < quads - 1)
            def _():
                @pl.when(j_own == 2)
                def _():
                    stage_copy().wait_recv()
                    both(ring_init(3, 1), "start")
                    both(ring_own(3, 1), "start")

                ring(3)

        ring(1)

        @pl.when(j_own == 0)
        def _():
            both(ring_own(0, 0), "start")

        ring(0)

        def gone(j):
            def hop_gone(hop, carry):
                def act(o, i, to):
                    for c in range(chunks):
                        @pl.when(hop < n - 1)
                        def _():
                            ring_copy(j, o, i, c, to).wait_send()

                        pass_copy(j, o, i, c).wait_send()

                hop_units(hop, act)
                return carry

            lax.fori_loop(1, n, hop_gone, 0)

        if quads > 1:
            @pl.when(q < quads - 1)
            def _():
                @pl.when(j_own == 2)
                def _():
                    both(ring_init(3, 1), "wait_send")
                    both(ring_own(3, 1), "wait_send")

                gone(3)

        gone(1)
        gone(0)

        @pl.when(j_own == 2)
        def _():
            both(e2_init(), "wait_send")
            both(e2_own(), "wait_send")
            l_gone(2)

        @pl.when(j_own == 0)
        def _():
            for j in range(2):
                both(ring_init(j, j), "wait_send")
                both(ring_own(j, j), "wait_send")
            l_gone(0)

        g_gone()

        @pl.when(j_own == 2)
        def _():
            mid_copy().wait_recv()

        @pl.when(j_own == 0)
        def _():
            for tile in range(tiles):
                for plane in range(2):
                    out_copy(tile, plane).wait_recv()

    @pl.when(core == 1)
    def _worker():
        @pl.when((j_own == 1) | jnp.logical_not(top))
        def _():
            stage_copy().start()

        @pl.when((j_own == 3) & top)
        def _():
            top_copy().start()

        send_g()

        @pl.when(j_own == 1)
        def _():
            send_l(1)

        if quads > 1:
            @pl.when((j_own == 3) & jnp.logical_not(top))
            def _():
                send_l(3)

        gbuf[r, j_own] = offset_in[...]

        def store_left(j, v, block):
            if rows == 192:
                left_out[j, v, 0:unit, :] = block[:, :LANES]
                for s in range(2):
                    left_out[j, v, unit:, s * 64:(s + 1) * 64] = block[
                        s * unit // 2:(s + 1) * unit // 2, LANES:
                    ]
            else:
                left_out[j, v] = block

        def place_left(j, d, i):
            at, low = d * rows, i * unit
            if rows == 192:
                left[low:low + unit, at:at + LANES] = left_in[j, d, i, 0:unit, :]
                for s in range(2):
                    left[low + s * unit // 2:low + (s + 1) * unit // 2, at + LANES:at + rows] = (
                        left_in[j, d, i, unit:, s * 64:(s + 1) * 64]
                    )
            else:
                left[low:low + unit, at:at + rows] = left_in[j, d, i]

        def send_left(j, v, d, i):
            @pl.when(d != r)
            def _():
                left_copy(j, d, i, v).start()

            @pl.when(d == r)
            def _():
                left_across(j, v, i).start()
                left_in[j, r, i] = left_out[j, v]

        def left_unit(o, i):
            v = place_of(o, i)
            product = lax.dot_general(
                e_half[2, unit_span(v, 0, unit), :], cov[3, 0:rows, :], CONTRACT_LAST,
                preferred_element_type=jnp.float32,
            )
            store_left(2, v, product.astype(jnp.bfloat16))
            send_left(2, v, o, i)

        def e2_copy(o, i, c, to):
            span = unit_span(place_of(o, i), c, CHUNK)
            return remote(
                e_half.at[2, span, :], e_half.at[2, span, :],
                e2_send.at[o, i, c], e2_recv.at[o, i, c], (t, to),
            )

        def e2_hop(hop, carry):
            def act(o, i, to):
                for c in range(chunks):
                    e2_copy(o, i, c, to).wait_recv()

                    @pl.when(hop < n - 1)
                    def _():
                        e2_copy(o, i, c, to).start()

            hop_units(hop, act)

            @pl.when(hop == LAG)
            def _():
                @pl.when(top)
                def _():
                    @pl.when(j_own == 1)
                    def _():
                        top_copy().wait_recv()

                    @pl.when(j_own == 3)
                    def _():
                        pltpu.make_async_copy(
                            cov_hbm, cov.at[3, pl.ds(0, rows), :], load_sems.at[0]
                        ).wait()

                for i in range(per):
                    @pl.when(plane_of(r, i) == p)
                    def _():
                        remote(
                            gain_in.at[pl.ds(0, unit), :],
                            e_half.at[2, unit_span(place_of(r, i), 0, unit), :],
                            e2_send.at[r, i, 0], e2_recv.at[r, i, 0], (t, right),
                        ).wait_recv()

                        @pl.when(top)
                        def _():
                            left_unit(r, i)

            @pl.when(top & (hop >= LAG))
            def _():
                first = jnp.where(hop == LAG, 1, hop)

                def left_hop(h, c):
                    hop_units(h, lambda o, i, to: left_unit(o, i))
                    return c

                lax.fori_loop(first, hop + 1, left_hop, 0)

            @pl.when(hop == LAG + 1)
            def _():
                for i in range(1, 4):
                    remote(
                        offset_in, gbuf.at[r, (j_own + i) % 4], g_send.at[0],
                        g_recv.at[(j_own + i) % 4], (partner, r),
                    ).wait_recv()

                def bundle(i, c):
                    g_bundle(other_row(i), r).start()
                    return c

                lax.fori_loop(1, n, bundle, 0)

            return carry

        lax.fori_loop(1, n, e2_hop, 0)

        def bundle_in(i, c):
            g_bundle(other_row(i), other_row(i)).wait_recv()
            return c

        lax.fori_loop(1, n, bundle_in, 0)
        total = gbuf[0]
        for i in range(1, n):
            total = total + gbuf[i]
        gsum[...] = total

        @pl.when(top)
        def _():
            cov[3, rows:, :] = jnp.broadcast_to(gsum[3], (PAD, size)).astype(jnp.bfloat16)

        first_step = jnp.where(top, 2, 3) if quads > 1 else 2
        started = jnp.where(top, 1, 0)

        def chain(k, carry):
            j = first_step - k

            if quads > 1:
                @pl.when(jnp.logical_not(top) & (j == 3))
                def _():
                    for tile in range(tiles):
                        for plane in range(2):
                            low_copy(tile, plane, p).wait_recv()

            @pl.when(k >= started)
            def _():
                @pl.when(j != 2)
                def _():
                    whole_arrival(j).wait_recv()

                share = units // LEFT_PARTS

                def left_part(g, c):
                    span = pl.ds(aligned(g * share * unit, share * unit), share * unit)
                    product = lax.dot_general(
                        e_half[j, span, :], cov[j + 1, 0:rows, :], CONTRACT_LAST,
                        preferred_element_type=jnp.float32,
                    ).astype(jnp.bfloat16)
                    for i in range(share):
                        store_left(j, g * share + i, product[i * unit:(i + 1) * unit])

                    def send(i, cc):
                        v = g * share + i
                        d, at = owner(v)
                        send_left(j, v, d, at)
                        return cc

                    lax.fori_loop(0, share, send, 0)
                    return c

                lax.fori_loop(0, LEFT_PARTS, left_part, 0)

            def pass_on(i, c):
                o = other_row(i)
                for at in range(per):
                    @pl.when(plane_of(r, at) == p)
                    def _():
                        left_pass(j, o, at).wait_recv()
                        left_pass(j, o, at).start()
                return c

            lax.fori_loop(1, n, pass_on, 0)

            def take(i, c):
                o = other_row(i)
                for at in range(per):
                    @pl.when(plane_of(r, at) != p)
                    def _():
                        left_pass(j, o, at).wait_recv()
                return c

            lax.fori_loop(0, n, take, 0)
            for d in range(n):
                for at in range(per):
                    place_left(j, d, at)
            left[rows:, :] = cov[j + 1, rows:, :]

            for tile in range(tiles):
                l_local(j, tile).wait()

            def right_part(g, c):
                wide = TILES_AT_ONCE * LANES
                product = lax.dot_general(
                    left[...], e_half[j, pl.ds(aligned(g * wide, wide), wide), :], CONTRACT_LAST,
                    preferred_element_type=jnp.float32,
                )
                for s in range(TILES_AT_ONCE):
                    tile = g * TILES_AT_ONCE + s
                    columns = nat_columns(tile, p)
                    block = product[:, s * LANES:(s + 1) * LANES]
                    cov[j, 0:rows, columns] = (
                        block[:rows] + l_in[j, :, half_columns(tile)].astype(jnp.float32)
                    ).astype(jnp.bfloat16)
                    cov[j, rows:, columns] = (
                        block[rows:] + gsum[j, :, columns]
                    ).astype(jnp.bfloat16)

                    @pl.when(j > 0)
                    def _():
                        x_copy(j, tile, p).start()

                    @pl.when(j == 0)
                    def _():
                        out_copy(tile, p).start()
                        if quads > 1:
                            @pl.when(q > 0)
                            def _():
                                for dest in range(2):
                                    low_copy(tile, p, dest).start()
                return c

            lax.fori_loop(0, tiles // TILES_AT_ONCE, right_part, 0)

            @pl.when(j > 0)
            def _():
                for tile in range(tiles):
                    x_copy(j, tile, 1 - p).wait_recv()

            @pl.when((j == 2) & (j_own == 3))
            def _():
                mid_copy().start()

            return carry

        lax.fori_loop(0, first_step + 1, chain, 0)

        out[...] = cov[j_own]

        def sent(k, carry):
            j = first_step - k

            def left_gone(v, c):
                d, at = owner(v)

                @pl.when(d != r)
                def _():
                    left_copy(j, d, at, v).wait_send()

                @pl.when(d == r)
                def _():
                    left_across(j, v, at).wait_send()
                return c

            lax.fori_loop(0, units, left_gone, 0)

            def pass_gone(i, c):
                o = other_row(i)
                for at in range(per):
                    @pl.when(plane_of(r, at) == p)
                    def _():
                        left_pass(j, o, at).wait_send()
                return c

            lax.fori_loop(1, n, pass_gone, 0)

            @pl.when(j > 0)
            def _():
                for tile in range(tiles):
                    x_copy(j, tile, p).wait_send()
            return carry

        lax.fori_loop(0, first_step + 1, sent, 0)

        def e2_gone(hop, carry):
            def act(o, i, to):
                for c in range(chunks):
                    e2_copy(o, i, c, to).wait_send()

            hop_units(hop, act)
            return carry

        lax.fori_loop(1, n - 1, e2_gone, 0)

        def bundle_gone(i, c):
            g_bundle(other_row(i), r).wait_send()
            return c

        lax.fori_loop(1, n, bundle_gone, 0)
        for tile in range(tiles):
            out_copy(tile, p).wait_send()
            if quads > 1:
                @pl.when(q > 0)
                def _():
                    for dest in range(2):
                        low_copy(tile, p, dest).wait_send()
        g_gone()

        @pl.when(j_own == 1)
        def _():
            l_gone(1)

        if quads > 1:
            @pl.when((j_own == 3) & jnp.logical_not(top))
            def _():
                l_gone(3)

        @pl.when((j_own == 1) | jnp.logical_not(top))
        def _():
            stage_copy().wait_send()

        @pl.when((j_own == 3) & top)
        def _():
            top_copy().wait_send()

        @pl.when(j_own == 3)
        def _():
            mid_copy().wait_send()


def shards(steps, n, smoother_gains, smoother_offsets, smoother_covs):
    own_gain = smoother_gains[0]
    own_cov = smoother_covs[0]
    rows, size = own_cov.shape
    start = lax.axis_index("rows") * rows
    offset_row = lax.dynamic_update_slice(
        jnp.zeros((1, size), jnp.float32), smoother_offsets.astype(jnp.float32), (0, start)
    )
    vmem = pl.BlockSpec(memory_space=pltpu.VMEM)
    hbm = pl.BlockSpec(memory_space=pltpu.HBM)
    gathers = 3 if steps == 4 else 4
    half = size // 2
    unit = unit_rows(rows)
    per = rows // unit
    chunks = unit // CHUNK
    tiles = half // LANES
    units = half // unit
    bf16 = jnp.bfloat16
    dma = pltpu.SemaphoreType.DMA
    both = pl.pallas_call(
        functools.partial(kernel, steps, n),
        out_shape=jax.ShapeDtypeStruct((rows + PAD, size), bf16),
        in_specs=[hbm, vmem, hbm],
        out_specs=vmem,
        scratch_shapes=[
            pltpu.VMEM((gathers, half, size), bf16),
            pltpu.VMEM((rows, size), bf16),
            pltpu.VMEM((gathers + 1, rows + PAD, size), bf16),
            pltpu.VMEM((gathers, rows, half), bf16),
            pltpu.VMEM((gathers, units) + folded(rows), bf16),
            pltpu.VMEM((gathers, n, per) + folded(rows), bf16),
            pltpu.VMEM((rows + PAD, size), bf16),
            pltpu.VMEM((n, 4, 1, size), jnp.float32),
            pltpu.VMEM((4, 1, size), jnp.float32),
            dma((n, per, chunks)),
            dma((n, per, chunks)),
            dma((gathers, n, per, chunks)),
            dma((gathers, n, per, chunks)),
            dma((gathers, n, per, chunks)),
            dma((gathers,)),
            dma((2, per, chunks + 1)),
            dma((2,)),
            dma((2, tiles)),
            dma((gathers, tiles)),
            dma((2,)),
            dma((1,)),
            dma((2,)),
            dma((4,)),
            dma((n,)),
            dma((n,)),
            dma((gathers, units)),
            dma((gathers, n, per)),
            dma((gathers, n, per)),
            dma((gathers, tiles)),
            dma((gathers, tiles)),
            dma((tiles,)),
            dma((2 * tiles,)),
            dma((2,)),
            dma((2, tiles)),
            dma((2 * tiles,)),
        ],
        compiler_params=pltpu.CompilerParams(
            collective_id=0, has_side_effects=True, vmem_limit_bytes=40 << 20
        ),
    )(pltpu.with_memory_space_constraint(own_gain, pltpu.HBM), offset_row, pltpu.with_memory_space_constraint(own_cov, pltpu.HBM))
    mean = lax.dynamic_slice(both, (rows, start), (1, rows))
    return mean, both[None, :rows]


def solution(mesh):
    in_specs = (P("tm", "rows", None), P("tm", "rows"), P("tm", "rows", None))
    out_specs = (P("tm", "rows"), P("tm", "rows", None))
    body = functools.partial(shards, mesh.shape["tm"], mesh.shape["rows"])
    return jax.shard_map(body, mesh=mesh, in_specs=in_specs, out_specs=out_specs, check_vma=False)
```

```python
import functools
import math

import jax
import jax.numpy as jnp
from jax import lax
from jax.experimental import pallas as pl
from jax.experimental.pallas import tpu as pltpu
from jax.sharding import PartitionSpec as P

MESH = pl.DeviceIdType.MESH
LANES = 128
PAD = 16
CHUNK = 32
GAIN_AT = 2
TOP_AT = 1
BUNDLE_AT = 2
BEHIND = 3
LAST_START = 3
SPREAD_AT = 1
LEFT_PARTS = 2
TILES_AT_ONCE = 2
CONTRACT_LAST = (((1,), (1,)), ((), ()))


def unit_rows(rows):
    return math.gcd(rows, LANES)


def share_sizes(rows, n):
    unit = unit_rows(rows)
    per, upt = rows // unit, LANES // unit
    planes = [[(per * d + i) // upt % 2 for i in range(per)] for d in range(n)]
    return sorted({row.count(x) for row in planes for x in range(2)} - {0})


def line_totals(rows, n):
    unit = unit_rows(rows)
    per, upt, spots = rows // unit, LANES // unit, n // 2
    beside, ahead = set(), set()
    for x in range(2):
        for lane in range(2):
            along = [
                sum((per * (at * 2 + lane) + i) // upt % 2 == x for i in range(per))
                for at in range(spots)
            ]
            beside.add(sum(along))
            for spot in range(spots):
                ahead.add(
                    (sum(along[:spot + 1]) if spot < spots - 1 else 0)
                    + (sum(along[spot:]) if spot > 0 else 0)
                )
    return sorted(beside), sorted(ahead)


def folded(rows):
    unit = unit_rows(rows)
    return (unit + unit // 2, LANES) if rows == 192 else (unit, rows)


def kernel(
    steps, n, gain_in, offset_in, cov_hbm, out,
    e_half, cov, l_in, left_out, left_in, left, gbuf, gsum,
    line_send, line_recv, pass_send, full_recv, init_send,
    l_send, l_recv, top_sems, load_sems, g_send, g_recv, gb_send, gb_recv,
    left_send, left_recv, across_recv, fwd_send, x_send, x_recv, out_sems, mid_sems,
    low_send, low_recv,
):
    t = lax.axis_index("tm")
    r = lax.axis_index("rows")
    spot, lane, spots = r // 2, r % 2, n // 2
    quads = steps // 4
    gathers = e_half.shape[0]
    q = t // 4
    b = q * 4
    j_own = t % 4
    p = j_own // 2
    core = t % 2
    top = q == quads - 1
    partner = b + 2 * (1 - p) + 1
    size = gain_in.shape[1]
    rows = size // n
    half = size // 2
    unit = unit_rows(rows)
    per = rows // unit
    upt = LANES // unit
    tiles = half // LANES
    units = half // unit
    chunks = unit // CHUNK
    picks = upt // 2
    counts = share_sizes(rows, n)

    def aligned(x, m):
        return pl.multiple_of(x, m)

    def remote(src, dst, send, recv, device):
        return pltpu.make_async_remote_copy(
            src_ref=src, dst_ref=dst, send_sem=send, recv_sem=recv,
            device_id=device, device_id_type=MESH,
        )

    def plane_of(d, i):
        return ((per * d + i) // upt) % 2

    def place_of(d, i):
        u = per * d + i
        return (u // upt // 2) * upt + u % upt

    def pick(o, w, k):
        start = per * o
        i = (upt * p + 2 * k + w - start + 2 * upt * n) % (2 * upt)
        return i

    mine = [plane_of(r, i) for i in range(per)]
    held = sum([1 - (x + p) % 2 for x in mine])
    first_held = (1 - (mine[0] + p) % 2) * 0 + ((mine[0] + p) % 2) * (per - held)
    first_other = (1 - (mine[0] + p) % 2) * held

    def owner(v):
        u = ((v // upt) * 2 + p) * upt + v % upt
        return u // per, u % per

    def unit_span(v, c, length):
        return pl.ds(aligned(v * unit + c * CHUNK, CHUNK), length)

    def nat_columns(tile, plane):
        return pl.ds(aligned((tile * 2 + plane) * LANES, LANES), LANES)

    def half_columns(tile):
        return pl.ds(aligned(tile * LANES, LANES), LANES)

    def other_row(i):
        return (r + i) % n

    barrier = pltpu.get_barrier_semaphore()

    def greet(tt, rr):
        pl.semaphore_signal(barrier, inc=1, device_id=(tt, rr), device_id_type=MESH)

    for i in range(1, 4):
        greet(b + (j_own + i) % 4, r)
    @pl.when(core == 1)
    def _():
        def greet_row(i, carry):
            greet(t, other_row(i))
            return carry

        lax.fori_loop(1, n, greet_row, 0)

    @pl.when(core == 0)
    def _():
        greet(t, spot * 2 + 1 - lane)
        greet(t + 1, spot * 2 + 1 - lane)

        @pl.when(spot > 0)
        def _():
            greet(t, r - 2)

        @pl.when(spot < spots - 1)
        def _():
            greet(t, r + 2)

    @pl.when(core == 1)
    def _():
        greet(t - 1, spot * 2 + 1 - lane)

    inner = (spot + spots - 1) // spots + (2 * spots - 2 - spot) // spots
    greetings = 3 + core * n + (1 - core) * (2 + inner)
    if quads > 1:
        for step in (-4, 4):
            near = (q * 4 + step >= 0) & (q * 4 + step < steps)

            @pl.when((core == 1) & near)
            def _():
                for i in (1, 3):
                    greet(b + step + i, r)

        greetings = greetings + core * 2 * (((q + quads - 1) // quads) + (2 * quads - 2 - q) // quads * 1)

    @pl.when(j_own == 3)
    def _():
        pltpu.make_async_copy(cov_hbm, cov.at[3, pl.ds(0, rows), :], load_sems.at[0]).start()

    pl.semaphore_wait(barrier, greetings)

    def slot_of(j):
        return 0 if j == 2 else (2 if j == 3 else j)

    def source(j, what):
        for i in range(per):
            x, v = plane_of(r, i), place_of(r, i)
            to = b + 2 * x + (1 if j == 2 else 0)
            for c in range(chunks):
                src = gain_in.at[pl.ds(i * unit + c * CHUNK, CHUNK), :]
                dst = e_half.at[j, unit_span(v, c, CHUNK), :]
                recv = line_recv.at[slot_of(j), v, c]

                def go():
                    remote(src, dst, init_send.at[0], recv, (to, r)).start()

                if j == 0:
                    @pl.when(to == t)
                    def _():
                        pltpu.make_async_copy(src, dst, recv).start()

                    pl.when(to != t)(go)
                else:
                    go()

    def source_gone(j):
        for count in ([per] if j else counts + [0]):
            @pl.when((per - held == count) | (j != 0))
            def _():
                if count:
                    block = gain_in.at[pl.ds(0, count * unit), :]
                    remote(
                        block, e_half.at[j, pl.ds(0, count * unit), :], init_send.at[0],
                        line_recv.at[0, 0, 0], (partner, r),
                    ).wait_send()

    def whole_arrival(j):
        return remote(e_half.at[j], e_half.at[j], init_send.at[0], full_recv.at[j], (t - 1, r))

    def unit_of(j, v):
        return e_half.at[j, unit_span(v, 0, unit), :]

    def line_units(d, act):
        for stream in range(2):
            at = spot - d if stream == 0 else spot + d
            inside = (at >= 0) & (at < spots)
            o = jnp.where(inside, at * 2 + lane, r)
            for w in range(2):
                for k in range(picks):
                    i = pick(o, w, k)
                    act(stream, inside & (i < per), place_of(o, i), w * picks + k)

    def onward(stream):
        return (spot < spots - 1) if stream == 0 else (spot > 0)

    def line_hop(j, d, with_pass):
        slot = slot_of(j)

        def forward(stream, c, v, which):
            span = unit_span(v, c, CHUNK)
            block = e_half.at[j, span, :]

            @pl.when(onward(stream))
            def _():
                remote(
                    block, block, line_send.at[slot, 0],
                    line_recv.at[slot, v, c], (t, r + 2 if stream == 0 else r - 2),
                ).start()

        def aside(stream, c, v, which):
            block = e_half.at[j, unit_span(v, c, CHUNK), :]
            if with_pass:
                if c == chunks - 1:
                    block = unit_of(j, v)
                    remote(
                        block, block, line_send.at[slot, 1], full_recv.at[j],
                        (t + 1, spot * 2 + 1 - lane),
                    ).start()
                    remote(
                        block, block, pass_send.at[slot], full_recv.at[j],
                        (t + 1, r),
                    ).start()
            else:
                remote(
                    block, block, line_send.at[slot, 1],
                    line_recv.at[slot, v, c], (t, spot * 2 + 1 - lane),
                ).start()

        for c in range(chunks):
            if isinstance(d, int):
                for w in range(2):
                    for k in range(picks):
                        i = pick(r, w, k)
                        v = place_of(r, i)
                        which = w * picks + k

                        @pl.when(i < per)
                        def _():
                            unit_chunk(j, v, c).wait_recv()
                            forward(0, c, v, which)
                            forward(1, c, v, which)
                            aside(0, c, v, which)
            else:
                def act(stream, ok, v, which):
                    @pl.when(ok)
                    def _():
                        unit_chunk(j, v, c).wait_recv()
                        forward(stream, c, v, which)
                        aside(stream, c, v, which)

                line_units(d, act)

    def unit_chunk(j, v, c):
        block = e_half.at[j, unit_span(v, c, CHUNK), :]
        return remote(
            block, block, init_send.at[0], line_recv.at[slot_of(j), v, c], (partner, r)
        )

    def line_gone(j, with_pass):
        slot = slot_of(j)
        along = [
            sum([1 - (plane_of(at * 2 + lane, i) + p) % 2 for i in range(per)])
            for at in range(spots)
        ]
        beside = sum(along)
        ahead = 0
        for at in range(spots):
            ahead = ahead + along[at] * jnp.where((at <= spot) & (spot < spots - 1), 1, 0)
            ahead = ahead + along[at] * jnp.where((at >= spot) & (spot > 0), 1, 0)

        def sent(count, total, sem):
            @pl.when(count == total)
            def _():
                block = e_half.at[j, pl.ds(0, total * unit), :]
                remote(block, block, sem, line_recv.at[0, 0, 0], (partner, r)).wait_send()

        for total in line_totals(rows, n)[0]:
            sent(beside, total, line_send.at[slot, 1])
            if with_pass:
                sent(beside, total, pass_send.at[slot])
        for total in line_totals(rows, n)[1]:
            sent(ahead, total, line_send.at[slot, 0])

    def l_copy(j, plane, tile):
        return remote(
            cov_hbm.at[:, nat_columns(tile, plane)],
            l_in.at[j, :, half_columns(tile)],
            l_send.at[plane], l_recv.at[j], (b + 2 * plane + 1, r),
        )

    def l_local(j, tile):
        return pltpu.make_async_copy(
            cov_hbm.at[:, nat_columns(tile, p)], l_in.at[j, :, half_columns(tile)],
            l_recv.at[j],
        )

    def l_whole(j, plane):
        return remote(
            l_in.at[j], l_in.at[j], l_send.at[plane], l_recv.at[j], (partner, r)
        )

    def top_copy():
        return remote(
            cov_hbm, cov.at[3, pl.ds(0, rows), :], top_sems.at[0], top_sems.at[1], (t - 2 * (2 * p - 1), r)
        )

    def g_copy(plane):
        return remote(
            offset_in, gbuf.at[r, j_own], g_send.at[plane], g_recv.at[0], (b + 2 * plane + 1, r)
        )

    def g_bundle(o, source):
        return remote(gbuf.at[source], gbuf.at[source], gb_send.at[0], gb_recv.at[0], (t, o))

    def left_copy(j, d, i, v):
        return remote(
            left_out.at[j, v], left_in.at[j, r, i], left_send.at[j], left_recv.at[j % 2, r], (t, d)
        )

    def left_across(j, v, i):
        return remote(
            left_out.at[j, v], left_in.at[j, r, i], left_send.at[j], across_recv.at[j % 2, r],
            (partner, r),
        )

    def left_block(j, o, start, count, recv):
        block = left_in.at[j, o, pl.ds(start, count)]
        return remote(block, block, fwd_send.at[j], recv, (partner, r))

    def left_sent(j):
        remote(
            left_out.at[j], left_out.at[j], left_send.at[j], left_recv.at[j % 2, r], (partner, r)
        ).wait_send()

    def left_pass(j, o, count):
        return left_block(j, o, first_held, count, across_recv.at[j % 2, o])

    def pass_sent(j, count):
        block = left_in.at[j, pl.ds(0, n - 1), pl.ds(0, count)]
        remote(block, block, fwd_send.at[j], across_recv.at[j % 2, r], (partner, r)).wait_send()

    def x_copy(j, tile, plane):
        columns = nat_columns(tile, plane)
        return remote(
            cov.at[j, :, columns], cov.at[j, :, columns], x_send.at[j], x_recv.at[j],
            (partner, r),
        )

    def x_whole(j):
        block = cov.at[j, :, pl.ds(0, half)]
        return remote(block, block, x_send.at[j], x_recv.at[j], (partner, r))

    def out_copy(tile, plane):
        columns = nat_columns(tile, plane)
        return remote(
            cov.at[0, :, columns], out.at[:, columns], out_sems.at[0], out_sems.at[1], (b, r),
        )

    def out_arrival():
        return remote(cov.at[0], out, out_sems.at[0], out_sems.at[1], (t + 1, r))

    def out_gone():
        block = cov.at[0, :, pl.ds(0, half)]
        remote(block, out.at[:, pl.ds(0, half)], out_sems.at[0], out_sems.at[1], (b, r)).wait_send()

    def mid_copy():
        return remote(cov.at[2], out, mid_sems.at[0], mid_sems.at[1], (b + 2, r))

    def low_copy(tile, plane, dest):
        columns = nat_columns(tile, plane)
        return remote(
            cov.at[0, :, columns], cov.at[gathers, :, columns], low_send.at[dest],
            low_recv.at[0], (b - 4 + 2 * dest + 1, r),
        )

    def both(copies, what):
        for copy in copies:
            getattr(copy, what)()

    def send_l(j):
        for plane in range(2):
            for tile in range(tiles):
                @pl.when(b + 2 * plane + 1 != t)
                def _():
                    l_copy(j, plane, tile).start()

                @pl.when(b + 2 * plane + 1 == t)
                def _():
                    l_local(j, tile).start()

    def l_gone(j):
        for plane in range(2):
            @pl.when(b + 2 * plane + 1 != t)
            def _():
                l_whole(j, plane).wait_send()

    def send_g():
        for plane in range(2):
            @pl.when(b + 2 * plane + 1 != t)
            def _():
                g_copy(plane).start()

    def g_gone():
        for plane in range(2):
            @pl.when(b + 2 * plane + 1 != t)
            def _():
                g_copy(plane).wait_send()

    @pl.when(core == 0)
    def _mover():
        @pl.when(j_own == 2)
        def _():
            source(2, "start")
            send_g()

        @pl.when(j_own == 0)
        def _():
            send_g()

        if quads > 1:
            @pl.when(q < quads - 1)
            def _():
                line_hop(3, 0, True)

                def hop3(d, carry):
                    line_hop(3, d, True)
                    return carry

                lax.fori_loop(1, spots, hop3, 0)

        line_hop(1, 0, True)

        def hop_step(d, carry):
            @pl.when((d == LAST_START) & (j_own == 0))
            def _():
                source(0, "start")

            @pl.when(d == SPREAD_AT)
            def _():
                @pl.when(j_own == 0)
                def _():
                    send_l(0)

                @pl.when(j_own == 2)
                def _():
                    send_l(2)

            @pl.when(d < spots)
            def _():
                line_hop(1, d, True)

            @pl.when(d == BEHIND)
            def _():
                line_hop(0, 0, True)

            @pl.when(d > BEHIND)
            def _():
                line_hop(0, d - BEHIND, True)

            return carry

        lax.fori_loop(1, spots + BEHIND, hop_step, 0)

        if quads > 1:
            @pl.when(q < quads - 1)
            def _():
                line_gone(3, True)

        line_gone(1, True)
        line_gone(0, True)

        @pl.when(j_own == 2)
        def _():
            source_gone(2)
            l_gone(2)

        @pl.when(j_own == 0)
        def _():
            source_gone(0)
            l_gone(0)

        g_gone()

        @pl.when(j_own == 2)
        def _():
            mid_copy().wait_recv()

        @pl.when(j_own == 0)
        def _():
            out_arrival().wait_recv()

    @pl.when(core == 1)
    def _worker():
        send_g()

        pltpu.make_async_copy(offset_in, gbuf.at[r, j_own], g_recv.at[1]).start()
        pltpu.make_async_copy(offset_in, gbuf.at[r, j_own], g_recv.at[1]).wait()

        def store_left(j, v, block):
            if rows == 192:
                left_out[j, v, 0:unit, :] = block[:, :LANES]
                for s in range(2):
                    left_out[j, v, unit:, s * 64:(s + 1) * 64] = block[
                        s * unit // 2:(s + 1) * unit // 2, LANES:
                    ]
            else:
                left_out[j, v] = block

        def place_left(j, d, i):
            at, low = d * rows, i * unit
            if rows == 192:
                left[low:low + unit, at:at + LANES] = left_in[j, d, i, 0:unit, :]
                for s in range(2):
                    left[low + s * unit // 2:low + (s + 1) * unit // 2, at + LANES:at + rows] = (
                        left_in[j, d, i, unit:, s * 64:(s + 1) * 64]
                    )
            else:
                left[low:low + unit, at:at + rows] = left_in[j, d, i]

        def send_left(j, v, d, i):
            @pl.when(d != r)
            def _():
                left_copy(j, d, i, v).start()

            @pl.when(d == r)
            def _():
                left_across(j, v, i).start()
                left_in[j, r, i] = left_out[j, v]

        def left_unit(o, i):
            v = place_of(o, i)
            product = lax.dot_general(
                e_half[2, unit_span(v, 0, unit), :], cov[3, 0:rows, :], CONTRACT_LAST,
                preferred_element_type=jnp.float32,
            )
            store_left(2, v, product.astype(jnp.bfloat16))
            send_left(2, v, o, i)

        def later(d):
            @pl.when((d == TOP_AT) & (j_own == 3) & top)
            def _():
                top_copy().start()

            @pl.when(d == GAIN_AT)
            def _():
                @pl.when(j_own == 1)
                def _():
                    source(1, "start")
                    send_l(1)

                if quads > 1:
                    @pl.when((j_own == 3) & jnp.logical_not(top))
                    def _():
                        source(3, "start")
                        send_l(3)

            @pl.when(d == BUNDLE_AT)
            def _():
                remote(
                    gbuf.at[r, pl.ds(0, 3)], gbuf.at[r, pl.ds(0, 3)], g_send.at[0], g_recv.at[0],
                    (partner, r),
                ).wait_recv()

                def bundle(i, c):
                    g_bundle(other_row(i), r).start()
                    return c

                lax.fori_loop(1, n, bundle, 0)

        line_hop(2, 0, False)

        def e2_hop(d, carry):
            line_hop(2, d, False)
            later(d)
            return carry

        lax.fori_loop(1, spots, e2_hop, 0)

        @pl.when(top)
        def _():
            @pl.when(j_own == 1)
            def _():
                top_copy().wait_recv()

            @pl.when(j_own == 3)
            def _():
                pltpu.make_async_copy(
                    cov_hbm, cov.at[3, pl.ds(0, rows), :], load_sems.at[0]
                ).wait()

            def own_lane(at, carry):
                for i in range(per):
                    @pl.when(plane_of(at * 2 + lane, i) == p)
                    def _():
                        left_unit(at * 2 + lane, i)
                return carry

            lax.fori_loop(0, spots, own_lane, 0)

        def other_lane(d, carry):
            for side in range(2):
                at = spot - d if side == 0 else spot + d
                o = at * 2 + 1 - lane
                for i in range(per):
                    @pl.when(
                        (at >= 0) & (at < spots) & ((side == 0) | (d > 0))
                        & (plane_of(o, i) == p)
                    )
                    def _():
                        for c in range(chunks):
                            unit_chunk(2, place_of(o, i), c).wait_recv()

                        @pl.when(top)
                        def _():
                            left_unit(o, i)
            return carry

        lax.fori_loop(0, spots, other_lane, 0)

        def bundles():
            return remote(
                gbuf.at[pl.ds(0, n - 1)], gbuf.at[pl.ds(0, n - 1)], gb_send.at[0], gb_recv.at[0],
                (partner, r),
            )

        bundles().wait_recv()
        for i in range(n):
            gsum[:, :, i * rows:(i + 1) * rows] = gbuf[i].astype(jnp.float32)

        @pl.when(top)
        def _():
            cov[3, rows:, :] = jnp.broadcast_to(gsum[3], (PAD, size)).astype(jnp.bfloat16)

        first_step = jnp.where(top, 2, 3) if quads > 1 else 2
        started = jnp.where(top, 1, 0)

        def chain(k, carry):
            j = first_step - k

            if quads > 1:
                @pl.when(jnp.logical_not(top) & (j == 3))
                def _():
                    remote(
                        cov.at[0], cov.at[gathers], low_send.at[0], low_recv.at[0], (partner, r)
                    ).wait_recv()

            @pl.when(k >= started)
            def _():
                @pl.when(j != 2)
                def _():
                    whole_arrival(j).wait_recv()

                share = units // LEFT_PARTS

                def left_part(g, c):
                    span = pl.ds(aligned(g * share * unit, share * unit), share * unit)
                    product = lax.dot_general(
                        e_half[j, span, :], cov[j + 1, 0:rows, :], CONTRACT_LAST,
                        preferred_element_type=jnp.float32,
                    ).astype(jnp.bfloat16)
                    for i in range(share):
                        store_left(j, g * share + i, product[i * unit:(i + 1) * unit])

                    def send(i, cc):
                        v = g * share + i
                        d, at = owner(v)
                        send_left(j, v, d, at)
                        return cc

                    lax.fori_loop(0, share, send, 0)
                    return c

                lax.fori_loop(0, LEFT_PARTS, left_part, 0)

            for count in counts:
                @pl.when(held == count)
                def _():
                    def pass_on(i, c):
                        o = other_row(i)
                        left_block(j, o, first_held, count, left_recv.at[j % 2, o]).wait_recv()
                        left_pass(j, o, count).start()
                        return c

                    lax.fori_loop(1, n, pass_on, 0)

            for count in counts:
                @pl.when(per - held == count)
                def _():
                    def take(i, c):
                        left_block(j, i, first_other, count, across_recv.at[j % 2, i]).wait_recv()
                        return c

                    lax.fori_loop(0, n, take, 0)

            for d in range(n):
                for at in range(per):
                    place_left(j, d, at)
            left[rows:, :] = cov[j + 1, rows:, :]

            l_whole(j, 0).wait_recv()

            def right_part(g, c):
                wide = TILES_AT_ONCE * LANES
                product = lax.dot_general(
                    left[...], e_half[j, pl.ds(aligned(g * wide, wide), wide), :], CONTRACT_LAST,
                    preferred_element_type=jnp.float32,
                )
                for s in range(TILES_AT_ONCE):
                    tile = g * TILES_AT_ONCE + s
                    columns = nat_columns(tile, p)
                    block = product[:, s * LANES:(s + 1) * LANES]
                    cov[j, 0:rows, columns] = (
                        block[:rows] + l_in[j, :, half_columns(tile)].astype(jnp.float32)
                    ).astype(jnp.bfloat16)
                    cov[j, rows:, columns] = (
                        block[rows:] + gsum[j, :, columns]
                    ).astype(jnp.bfloat16)

                    @pl.when(j > 0)
                    def _():
                        x_copy(j, tile, p).start()

                    @pl.when(j == 0)
                    def _():
                        out_copy(tile, p).start()
                        if quads > 1:
                            @pl.when(q > 0)
                            def _():
                                for dest in range(2):
                                    low_copy(tile, p, dest).start()
                return c

            lax.fori_loop(0, tiles // TILES_AT_ONCE, right_part, 0)

            @pl.when(j > 0)
            def _():
                x_whole(j).wait_recv()

            @pl.when((j == 2) & (j_own == 3))
            def _():
                mid_copy().start()

            return carry

        lax.fori_loop(0, first_step + 1, chain, 0)

        out[...] = cov[j_own]

        def sent(k, carry):
            j = first_step - k

            left_sent(j)
            for count in counts:
                @pl.when(held == count)
                def _():
                    pass_sent(j, count)

            @pl.when(j > 0)
            def _():
                x_whole(j).wait_send()

            return carry

        lax.fori_loop(0, first_step + 1, sent, 0)

        line_gone(2, False)
        bundles().wait_send()
        out_gone()
        if quads > 1:
            @pl.when(q > 0)
            def _():
                for dest in range(2):
                    remote(
                        cov.at[0, :, pl.ds(0, half)], cov.at[gathers, :, pl.ds(0, half)],
                        low_send.at[dest], low_recv.at[0], (partner, r),
                    ).wait_send()
        g_gone()

        @pl.when(j_own == 1)
        def _():
            source_gone(1)
            l_gone(1)

        if quads > 1:
            @pl.when((j_own == 3) & jnp.logical_not(top))
            def _():
                source_gone(3)
                l_gone(3)

        @pl.when((j_own == 3) & top)
        def _():
            top_copy().wait_send()

        @pl.when(j_own == 3)
        def _():
            mid_copy().wait_send()


def shards(steps, n, smoother_gains, smoother_offsets, smoother_covs):
    own_gain = smoother_gains[0]
    own_cov = smoother_covs[0]
    rows, size = own_cov.shape
    start = lax.axis_index("rows") * rows
    vmem = pl.BlockSpec(memory_space=pltpu.VMEM)
    hbm = pl.BlockSpec(memory_space=pltpu.HBM)
    gathers = 3 if steps == 4 else 4
    half = size // 2
    unit = unit_rows(rows)
    per = rows // unit
    chunks = unit // CHUNK
    tiles = half // LANES
    units = half // unit
    upt = LANES // unit
    slots = 2 if steps == 4 else 3
    bf16 = jnp.bfloat16
    dma = pltpu.SemaphoreType.DMA
    both = pl.pallas_call(
        functools.partial(kernel, steps, n),
        out_shape=jax.ShapeDtypeStruct((rows + PAD, size), bf16),
        in_specs=[hbm, hbm, hbm],
        out_specs=vmem,
        scratch_shapes=[
            pltpu.VMEM((gathers, half, size), bf16),
            pltpu.VMEM((gathers + 1, rows + PAD, size), bf16),
            pltpu.VMEM((gathers, rows, half), bf16),
            pltpu.VMEM((gathers, units) + folded(rows), bf16),
            pltpu.VMEM((gathers, n, per) + folded(rows), bf16),
            pltpu.VMEM((rows + PAD, size), bf16),
            pltpu.VMEM((n, 4, 1, rows), bf16),
            pltpu.VMEM((4, 1, size), jnp.float32),
            dma((slots, 2)),
            dma((slots, units, chunks)),
            dma((slots,)),
            dma((gathers,)),
            dma((1,)),
            dma((2,)),
            dma((gathers,)),
            dma((2,)),
            dma((1,)),
            dma((2,)),
            dma((2,)),
            dma((1,)),
            dma((1,)),
            dma((gathers,)),
            dma((2, n)),
            dma((2, n)),
            dma((gathers,)),
            dma((gathers,)),
            dma((gathers,)),
            dma((2,)),
            dma((2,)),
            dma((2,)),
            dma((1,)),
        ],
        compiler_params=pltpu.CompilerParams(
            collective_id=0, has_side_effects=True, vmem_limit_bytes=40 << 20
        ),
    )(pltpu.with_memory_space_constraint(own_gain, pltpu.HBM), pltpu.with_memory_space_constraint(smoother_offsets, pltpu.HBM), pltpu.with_memory_space_constraint(own_cov, pltpu.HBM))
    mean = lax.dynamic_slice(both, (rows, start), (1, rows))
    return mean, both[None, :rows]


def solution(mesh):
    in_specs = (P("tm", "rows", None), P("tm", "rows"), P("tm", "rows", None))
    out_specs = (P("tm", "rows"), P("tm", "rows", None))
    body = functools.partial(shards, mesh.shape["tm"], mesh.shape["rows"])
    return jax.shard_map(body, mesh=mesh, in_specs=in_specs, out_specs=out_specs, check_vma=False)
```

```python
import functools
import math

import jax
import jax.numpy as jnp
from jax import lax
from jax.experimental import pallas as pl
from jax.experimental.pallas import tpu as pltpu
from jax.sharding import PartitionSpec as P

MESH = pl.DeviceIdType.MESH
LANES = 128
PAD = 16
CHUNK = 32
GAIN_AT = 2
TOP_AT = 1
BUNDLE_AT = 2
BEHIND = 3
SPREAD_AT = 1
LEFT_PARTS = 2
TILES_AT_ONCE = 2
CONTRACT_LAST = (((1,), (1,)), ((), ()))


def unit_rows(rows):
    return math.gcd(rows, LANES)


def share_sizes(rows, n):
    unit = unit_rows(rows)
    per, upt = rows // unit, LANES // unit
    planes = [[(per * d + i) // upt % 2 for i in range(per)] for d in range(n)]
    return sorted({row.count(x) for row in planes for x in range(2)} - {0})


def line_totals(rows, n):
    unit = unit_rows(rows)
    per, upt, spots = rows // unit, LANES // unit, n // 2
    beside, ahead = set(), set()
    for x in range(2):
        for lane in range(2):
            along = [
                sum((per * (at * 2 + lane) + i) // upt % 2 == x for i in range(per))
                for at in range(spots)
            ]
            beside.add(sum(along))
            for spot in range(spots):
                ahead.add(
                    (sum(along[:spot + 1]) if spot < spots - 1 else 0)
                    + (sum(along[spot:]) if spot > 0 else 0)
                )
    return sorted(beside), sorted(ahead)


def folded(rows):
    unit = unit_rows(rows)
    return (unit + unit // 2, LANES) if rows == 192 else (unit, rows)


def kernel(
    steps, n, gain_in, offset_in, cov_hbm, out,
    e_half, cov, l_in, left_out, left_in, left, gbuf, gsum,
    line_send, line_recv, pass_send, full_recv, init_send,
    l_send, l_recv, top_sems, load_sems, g_send, g_recv, gb_send, gb_recv,
    left_send, left_recv, across_recv, fwd_send, x_send, x_recv, out_sems, mid_sems,
    low_send, low_recv,
):
    t = lax.axis_index("tm")
    r = lax.axis_index("rows")
    spot, lane, spots = r // 2, r % 2, n // 2
    quads = steps // 4
    gathers = e_half.shape[0]
    q = t // 4
    b = q * 4
    j_own = t % 4
    p = j_own // 2
    core = t % 2
    top = q == quads - 1
    partner = b + 2 * (1 - p) + 1
    size = gain_in.shape[1]
    rows = size // n
    half = size // 2
    unit = unit_rows(rows)
    per = rows // unit
    upt = LANES // unit
    tiles = half // LANES
    units = half // unit
    chunks = unit // CHUNK
    picks = upt // 2
    counts = share_sizes(rows, n)

    def aligned(x, m):
        return pl.multiple_of(x, m)

    def remote(src, dst, send, recv, device):
        return pltpu.make_async_remote_copy(
            src_ref=src, dst_ref=dst, send_sem=send, recv_sem=recv,
            device_id=device, device_id_type=MESH,
        )

    def plane_of(d, i):
        return ((per * d + i) // upt) % 2

    def place_of(d, i):
        u = per * d + i
        return (u // upt // 2) * upt + u % upt

    def pick(o, w, k):
        start = per * o
        i = (upt * p + 2 * k + w - start + 2 * upt * n) % (2 * upt)
        return i

    mine = [plane_of(r, i) for i in range(per)]
    held = sum([1 - (x + p) % 2 for x in mine])
    first_held = (1 - (mine[0] + p) % 2) * 0 + ((mine[0] + p) % 2) * (per - held)
    first_other = (1 - (mine[0] + p) % 2) * held

    def owner(v):
        u = ((v // upt) * 2 + p) * upt + v % upt
        return u // per, u % per

    def unit_span(v, c, length):
        return pl.ds(aligned(v * unit + c * CHUNK, CHUNK), length)

    def nat_columns(tile, plane):
        return pl.ds(aligned((tile * 2 + plane) * LANES, LANES), LANES)

    def half_columns(tile):
        return pl.ds(aligned(tile * LANES, LANES), LANES)

    def other_row(i):
        return (r + i) % n

    barrier = pltpu.get_barrier_semaphore()

    def greet(tt, rr):
        pl.semaphore_signal(barrier, inc=1, device_id=(tt, rr), device_id_type=MESH)

    for i in range(1, 4):
        greet(b + (j_own + i) % 4, r)
    @pl.when(core == 1)
    def _():
        def greet_row(i, carry):
            greet(t, other_row(i))
            return carry

        lax.fori_loop(1, n, greet_row, 0)

    @pl.when(core == 0)
    def _():
        greet(t, spot * 2 + 1 - lane)
        greet(t + 1, spot * 2 + 1 - lane)

        @pl.when(spot > 0)
        def _():
            greet(t, r - 2)

        @pl.when(spot < spots - 1)
        def _():
            greet(t, r + 2)

    @pl.when(core == 1)
    def _():
        greet(t - 1, spot * 2 + 1 - lane)

    inner = (spot + spots - 1) // spots + (2 * spots - 2 - spot) // spots
    greetings = 3 + core * n + (1 - core) * (2 + inner)
    if quads > 1:
        for step in (-4, 4):
            near = (q * 4 + step >= 0) & (q * 4 + step < steps)

            @pl.when((core == 1) & near)
            def _():
                for i in (1, 3):
                    greet(b + step + i, r)

        greetings = greetings + core * 2 * (((q + quads - 1) // quads) + (2 * quads - 2 - q) // quads * 1)

    @pl.when(j_own == 3)
    def _():
        pltpu.make_async_copy(cov_hbm, cov.at[3, pl.ds(0, rows), :], load_sems.at[0]).start()

    pl.semaphore_wait(barrier, greetings)

    def slot_of(j):
        return 0 if j == 2 else (2 if j == 3 else j)

    def source(j, what):
        for i in range(per):
            x, v = plane_of(r, i), place_of(r, i)
            to = b + 2 * x + (1 if j == 2 else 0)
            for c in range(chunks):
                src = gain_in.at[pl.ds(i * unit + c * CHUNK, CHUNK), :]
                dst = e_half.at[j, unit_span(v, c, CHUNK), :]
                recv = line_recv.at[slot_of(j), v, c]

                def go():
                    remote(src, dst, init_send.at[0], recv, (to, r)).start()

                if j == 0:
                    @pl.when(to == t)
                    def _():
                        pltpu.make_async_copy(src, dst, recv).start()

                    pl.when(to != t)(go)
                else:
                    go()

    def source_gone(j):
        for count in ([per] if j else counts + [0]):
            @pl.when((per - held == count) | (j != 0))
            def _():
                if count:
                    block = gain_in.at[pl.ds(0, count * unit), :]
                    remote(
                        block, e_half.at[j, pl.ds(0, count * unit), :], init_send.at[0],
                        line_recv.at[0, 0, 0], (partner, r),
                    ).wait_send()

    def whole_arrival(j):
        return remote(e_half.at[j], e_half.at[j], init_send.at[0], full_recv.at[j], (t - 1, r))

    def unit_of(j, v):
        return e_half.at[j, unit_span(v, 0, unit), :]

    def line_units(d, act):
        for stream in range(2):
            at = spot - d if stream == 0 else spot + d
            inside = (at >= 0) & (at < spots)
            o = jnp.where(inside, at * 2 + lane, r)
            for w in range(2):
                for k in range(picks):
                    i = pick(o, w, k)
                    act(stream, inside & (i < per), place_of(o, i), w * picks + k)

    def onward(stream):
        return (spot < spots - 1) if stream == 0 else (spot > 0)

    def line_hop(j, d, with_pass):
        slot = slot_of(j)

        def forward(stream, c, v, which):
            span = unit_span(v, c, CHUNK)
            block = e_half.at[j, span, :]

            @pl.when(onward(stream))
            def _():
                remote(
                    block, block, line_send.at[slot, 0],
                    line_recv.at[slot, v, c], (t, r + 2 if stream == 0 else r - 2),
                ).start()

        def aside(stream, c, v, which):
            block = e_half.at[j, unit_span(v, c, CHUNK), :]
            if with_pass:
                remote(
                    block, block, line_send.at[slot, 1], full_recv.at[j],
                    (t + 1, spot * 2 + 1 - lane),
                ).start()
                if c == chunks - 1:
                    block = unit_of(j, v)
                    remote(
                        block, block, pass_send.at[slot], full_recv.at[j],
                        (t + 1, r),
                    ).start()
            else:
                remote(
                    block, block, line_send.at[slot, 1],
                    line_recv.at[slot, v, c], (t, spot * 2 + 1 - lane),
                ).start()

        for c in range(chunks):
            if isinstance(d, int):
                for w in range(2):
                    for k in range(picks):
                        i = pick(r, w, k)
                        v = place_of(r, i)
                        which = w * picks + k

                        @pl.when(i < per)
                        def _():
                            unit_chunk(j, v, c).wait_recv()
                            forward(0, c, v, which)
                            forward(1, c, v, which)
                            aside(0, c, v, which)
            else:
                def act(stream, ok, v, which):
                    @pl.when(ok)
                    def _():
                        unit_chunk(j, v, c).wait_recv()
                        forward(stream, c, v, which)
                        aside(stream, c, v, which)

                line_units(d, act)

    def unit_chunk(j, v, c):
        block = e_half.at[j, unit_span(v, c, CHUNK), :]
        return remote(
            block, block, init_send.at[0], line_recv.at[slot_of(j), v, c], (partner, r)
        )

    def line_gone(j, with_pass):
        slot = slot_of(j)
        along = [
            sum([1 - (plane_of(at * 2 + lane, i) + p) % 2 for i in range(per)])
            for at in range(spots)
        ]
        beside = sum(along)
        ahead = 0
        for at in range(spots):
            ahead = ahead + along[at] * jnp.where((at <= spot) & (spot < spots - 1), 1, 0)
            ahead = ahead + along[at] * jnp.where((at >= spot) & (spot > 0), 1, 0)

        def sent(count, total, sem):
            @pl.when(count == total)
            def _():
                block = e_half.at[j, pl.ds(0, total * unit), :]
                remote(block, block, sem, line_recv.at[0, 0, 0], (partner, r)).wait_send()

        for total in line_totals(rows, n)[0]:
            sent(beside, total, line_send.at[slot, 1])
            if with_pass:
                sent(beside, total, pass_send.at[slot])
        for total in line_totals(rows, n)[1]:
            sent(ahead, total, line_send.at[slot, 0])

    def l_copy(j, plane, tile):
        return remote(
            cov_hbm.at[:, nat_columns(tile, plane)],
            l_in.at[j, :, half_columns(tile)],
            l_send.at[plane], l_recv.at[j], (b + 2 * plane + 1, r),
        )

    def l_local(j, tile):
        return pltpu.make_async_copy(
            cov_hbm.at[:, nat_columns(tile, p)], l_in.at[j, :, half_columns(tile)],
            l_recv.at[j],
        )

    def l_whole(j, plane):
        return remote(
            l_in.at[j], l_in.at[j], l_send.at[plane], l_recv.at[j], (partner, r)
        )

    def top_copy():
        return remote(
            cov_hbm, cov.at[3, pl.ds(0, rows), :], top_sems.at[0], top_sems.at[1], (t - 2 * (2 * p - 1), r)
        )

    def g_copy(plane):
        return remote(
            offset_in, gbuf.at[r, j_own], g_send.at[plane], g_recv.at[0], (b + 2 * plane + 1, r)
        )

    def g_bundle(o, source):
        return remote(gbuf.at[source], gbuf.at[source], gb_send.at[0], gb_recv.at[0], (t, o))

    def left_copy(j, d, i, v):
        return remote(
            left_out.at[j, v], left_in.at[j, r, i], left_send.at[j], left_recv.at[j % 2, r], (t, d)
        )

    def left_across(j, v, i):
        return remote(
            left_out.at[j, v], left_in.at[j, r, i], left_send.at[j], across_recv.at[j % 2, r],
            (partner, r),
        )

    def left_block(j, o, start, count, recv):
        block = left_in.at[j, o, pl.ds(start, count)]
        return remote(block, block, fwd_send.at[j], recv, (partner, r))

    def left_sent(j):
        remote(
            left_out.at[j], left_out.at[j], left_send.at[j], left_recv.at[j % 2, r], (partner, r)
        ).wait_send()

    def left_pass(j, o, count):
        return left_block(j, o, first_held, count, across_recv.at[j % 2, o])

    def pass_sent(j, count):
        block = left_in.at[j, pl.ds(0, n - 1), pl.ds(0, count)]
        remote(block, block, fwd_send.at[j], across_recv.at[j % 2, r], (partner, r)).wait_send()

    def x_copy(j, tile, plane):
        columns = nat_columns(tile, plane)
        return remote(
            cov.at[j, :, columns], cov.at[j, :, columns], x_send.at[j], x_recv.at[j],
            (partner, r),
        )

    def x_whole(j):
        block = cov.at[j, :, pl.ds(0, half)]
        return remote(block, block, x_send.at[j], x_recv.at[j], (partner, r))

    def out_copy(tile, plane):
        columns = nat_columns(tile, plane)
        return remote(
            cov.at[0, :, columns], out.at[:, columns], out_sems.at[0], out_sems.at[1], (b, r),
        )

    def out_arrival():
        return remote(cov.at[0], out, out_sems.at[0], out_sems.at[1], (t + 1, r))

    def out_gone():
        block = cov.at[0, :, pl.ds(0, half)]
        remote(block, out.at[:, pl.ds(0, half)], out_sems.at[0], out_sems.at[1], (b, r)).wait_send()

    def mid_copy():
        return remote(cov.at[2], out, mid_sems.at[0], mid_sems.at[1], (b + 2, r))

    def low_copy(tile, plane, dest):
        columns = nat_columns(tile, plane)
        return remote(
            cov.at[0, :, columns], cov.at[gathers, :, columns], low_send.at[dest],
            low_recv.at[0], (b - 4 + 2 * dest + 1, r),
        )

    def both(copies, what):
        for copy in copies:
            getattr(copy, what)()

    def send_l(j):
        for plane in range(2):
            for tile in range(tiles):
                @pl.when(b + 2 * plane + 1 != t)
                def _():
                    l_copy(j, plane, tile).start()

                @pl.when(b + 2 * plane + 1 == t)
                def _():
                    l_local(j, tile).start()

    def l_gone(j):
        for plane in range(2):
            @pl.when(b + 2 * plane + 1 != t)
            def _():
                l_whole(j, plane).wait_send()

    def send_g():
        for plane in range(2):
            @pl.when(b + 2 * plane + 1 != t)
            def _():
                g_copy(plane).start()

    def g_gone():
        for plane in range(2):
            @pl.when(b + 2 * plane + 1 != t)
            def _():
                g_copy(plane).wait_send()

    @pl.when(core == 0)
    def _mover():
        @pl.when(j_own == 2)
        def _():
            source(2, "start")
            send_g()

        @pl.when(j_own == 0)
        def _():
            send_g()
            source(0, "start")
            send_l(0)

        if quads > 1:
            @pl.when(q < quads - 1)
            def _():
                line_hop(3, 0, True)

                def hop3(d, carry):
                    line_hop(3, d, True)
                    return carry

                lax.fori_loop(1, spots, hop3, 0)

        line_hop(1, 0, True)

        def hop_step(d, carry):
            @pl.when(d == SPREAD_AT)
            def _():
                @pl.when(j_own == 2)
                def _():
                    send_l(2)

            @pl.when(d < spots)
            def _():
                line_hop(1, d, True)

            @pl.when(d == BEHIND)
            def _():
                line_hop(0, 0, True)

            @pl.when(d > BEHIND)
            def _():
                line_hop(0, d - BEHIND, True)

            return carry

        lax.fori_loop(1, spots + BEHIND, hop_step, 0)

        if quads > 1:
            @pl.when(q < quads - 1)
            def _():
                line_gone(3, True)

        line_gone(1, True)
        line_gone(0, True)

        @pl.when(j_own == 2)
        def _():
            source_gone(2)
            l_gone(2)

        @pl.when(j_own == 0)
        def _():
            source_gone(0)
            l_gone(0)

        g_gone()

        @pl.when(j_own == 2)
        def _():
            mid_copy().wait_recv()

        @pl.when(j_own == 0)
        def _():
            out_arrival().wait_recv()

    @pl.when(core == 1)
    def _worker():
        send_g()

        pltpu.make_async_copy(offset_in, gbuf.at[r, j_own], g_recv.at[1]).start()
        pltpu.make_async_copy(offset_in, gbuf.at[r, j_own], g_recv.at[1]).wait()

        def store_left(j, v, block):
            if rows == 192:
                left_out[j, v, 0:unit, :] = block[:, :LANES]
                for s in range(2):
                    left_out[j, v, unit:, s * 64:(s + 1) * 64] = block[
                        s * unit // 2:(s + 1) * unit // 2, LANES:
                    ]
            else:
                left_out[j, v] = block

        def place_left(j, d, i):
            at, low = d * rows, i * unit
            if rows == 192:
                left[low:low + unit, at:at + LANES] = left_in[j, d, i, 0:unit, :]
                for s in range(2):
                    left[low + s * unit // 2:low + (s + 1) * unit // 2, at + LANES:at + rows] = (
                        left_in[j, d, i, unit:, s * 64:(s + 1) * 64]
                    )
            else:
                left[low:low + unit, at:at + rows] = left_in[j, d, i]

        def send_left(j, v, d, i):
            @pl.when(d != r)
            def _():
                left_copy(j, d, i, v).start()

            @pl.when(d == r)
            def _():
                left_across(j, v, i).start()
                left_in[j, r, i] = left_out[j, v]

        def left_unit(o, i):
            v = place_of(o, i)
            product = lax.dot_general(
                e_half[2, unit_span(v, 0, unit), :], cov[3, 0:rows, :], CONTRACT_LAST,
                preferred_element_type=jnp.float32,
            )
            store_left(2, v, product.astype(jnp.bfloat16))
            send_left(2, v, o, i)

        def later(d):
            @pl.when((d == TOP_AT) & (j_own == 3) & top)
            def _():
                top_copy().start()

            @pl.when((d == 1) & (j_own == 1))
            def _():
                send_l(1)

            @pl.when(d == GAIN_AT)
            def _():
                @pl.when(j_own == 1)
                def _():
                    source(1, "start")

                if quads > 1:
                    @pl.when((j_own == 3) & jnp.logical_not(top))
                    def _():
                        source(3, "start")
                        send_l(3)

            @pl.when(d == BUNDLE_AT)
            def _():
                remote(
                    gbuf.at[r, pl.ds(0, 3)], gbuf.at[r, pl.ds(0, 3)], g_send.at[0], g_recv.at[0],
                    (partner, r),
                ).wait_recv()

                def bundle(i, c):
                    g_bundle(other_row(i), r).start()
                    return c

                lax.fori_loop(1, n, bundle, 0)

        line_hop(2, 0, False)

        def e2_hop(d, carry):
            line_hop(2, d, False)
            later(d)
            return carry

        lax.fori_loop(1, spots, e2_hop, 0)

        @pl.when(top)
        def _():
            @pl.when(j_own == 1)
            def _():
                top_copy().wait_recv()

            @pl.when(j_own == 3)
            def _():
                pltpu.make_async_copy(
                    cov_hbm, cov.at[3, pl.ds(0, rows), :], load_sems.at[0]
                ).wait()

            def own_lane(at, carry):
                for i in range(per):
                    @pl.when(plane_of(at * 2 + lane, i) == p)
                    def _():
                        left_unit(at * 2 + lane, i)
                return carry

            lax.fori_loop(0, spots, own_lane, 0)

        def other_lane(d, carry):
            for side in range(2):
                at = spot - d if side == 0 else spot + d
                o = at * 2 + 1 - lane
                for i in range(per):
                    @pl.when(
                        (at >= 0) & (at < spots) & ((side == 0) | (d > 0))
                        & (plane_of(o, i) == p)
                    )
                    def _():
                        for c in range(chunks):
                            unit_chunk(2, place_of(o, i), c).wait_recv()

                        @pl.when(top)
                        def _():
                            left_unit(o, i)
            return carry

        lax.fori_loop(0, spots, other_lane, 0)

        def bundles():
            return remote(
                gbuf.at[pl.ds(0, n - 1)], gbuf.at[pl.ds(0, n - 1)], gb_send.at[0], gb_recv.at[0],
                (partner, r),
            )

        bundles().wait_recv()
        for i in range(n):
            gsum[:, :, i * rows:(i + 1) * rows] = gbuf[i].astype(jnp.float32)

        @pl.when(top)
        def _():
            cov[3, rows:, :] = jnp.broadcast_to(gsum[3], (PAD, size)).astype(jnp.bfloat16)

        first_step = jnp.where(top, 2, 3) if quads > 1 else 2
        started = jnp.where(top, 1, 0)

        def chain(k, carry):
            j = first_step - k

            if quads > 1:
                @pl.when(jnp.logical_not(top) & (j == 3))
                def _():
                    remote(
                        cov.at[0], cov.at[gathers], low_send.at[0], low_recv.at[0], (partner, r)
                    ).wait_recv()

            @pl.when(k >= started)
            def _():
                @pl.when(j != 2)
                def _():
                    whole_arrival(j).wait_recv()

                share = units // LEFT_PARTS

                def left_part(g, c):
                    span = pl.ds(aligned(g * share * unit, share * unit), share * unit)
                    product = lax.dot_general(
                        e_half[j, span, :], cov[j + 1, 0:rows, :], CONTRACT_LAST,
                        preferred_element_type=jnp.float32,
                    ).astype(jnp.bfloat16)
                    for i in range(share):
                        store_left(j, g * share + i, product[i * unit:(i + 1) * unit])

                    def send(i, cc):
                        v = g * share + i
                        d, at = owner(v)
                        send_left(j, v, d, at)
                        return cc

                    lax.fori_loop(0, share, send, 0)
                    return c

                lax.fori_loop(0, LEFT_PARTS, left_part, 0)

            for count in counts:
                @pl.when(held == count)
                def _():
                    def pass_on(i, c):
                        o = other_row(i)
                        left_block(j, o, first_held, count, left_recv.at[j % 2, o]).wait_recv()
                        left_pass(j, o, count).start()
                        return c

                    lax.fori_loop(1, n, pass_on, 0)

            for count in counts:
                @pl.when(per - held == count)
                def _():
                    def take(i, c):
                        left_block(j, i, first_other, count, across_recv.at[j % 2, i]).wait_recv()
                        return c

                    lax.fori_loop(0, n, take, 0)

            for d in range(n):
                for at in range(per):
                    place_left(j, d, at)
            left[rows:, :] = cov[j + 1, rows:, :]

            l_whole(j, 0).wait_recv()

            def right_part(g, c):
                wide = TILES_AT_ONCE * LANES
                product = lax.dot_general(
                    left[...], e_half[j, pl.ds(aligned(g * wide, wide), wide), :], CONTRACT_LAST,
                    preferred_element_type=jnp.float32,
                )
                for s in range(TILES_AT_ONCE):
                    tile = g * TILES_AT_ONCE + s
                    columns = nat_columns(tile, p)
                    block = product[:, s * LANES:(s + 1) * LANES]
                    cov[j, 0:rows, columns] = (
                        block[:rows] + l_in[j, :, half_columns(tile)].astype(jnp.float32)
                    ).astype(jnp.bfloat16)
                    cov[j, rows:, columns] = (
                        block[rows:] + gsum[j, :, columns]
                    ).astype(jnp.bfloat16)

                    @pl.when(j > 0)
                    def _():
                        x_copy(j, tile, p).start()

                    @pl.when(j == 0)
                    def _():
                        out_copy(tile, p).start()
                        if quads > 1:
                            @pl.when(q > 0)
                            def _():
                                for dest in range(2):
                                    low_copy(tile, p, dest).start()
                return c

            lax.fori_loop(0, tiles // TILES_AT_ONCE, right_part, 0)

            @pl.when(j > 0)
            def _():
                x_whole(j).wait_recv()

            @pl.when((j == 2) & (j_own == 3))
            def _():
                mid_copy().start()

            return carry

        lax.fori_loop(0, first_step + 1, chain, 0)

        out[...] = cov[j_own]

        def sent(k, carry):
            j = first_step - k

            left_sent(j)
            for count in counts:
                @pl.when(held == count)
                def _():
                    pass_sent(j, count)

            @pl.when(j > 0)
            def _():
                x_whole(j).wait_send()

            return carry

        lax.fori_loop(0, first_step + 1, sent, 0)

        line_gone(2, False)
        bundles().wait_send()
        out_gone()
        if quads > 1:
            @pl.when(q > 0)
            def _():
                for dest in range(2):
                    remote(
                        cov.at[0, :, pl.ds(0, half)], cov.at[gathers, :, pl.ds(0, half)],
                        low_send.at[dest], low_recv.at[0], (partner, r),
                    ).wait_send()
        g_gone()

        @pl.when(j_own == 1)
        def _():
            source_gone(1)
            l_gone(1)

        if quads > 1:
            @pl.when((j_own == 3) & jnp.logical_not(top))
            def _():
                source_gone(3)
                l_gone(3)

        @pl.when((j_own == 3) & top)
        def _():
            top_copy().wait_send()

        @pl.when(j_own == 3)
        def _():
            mid_copy().wait_send()


def shards(steps, n, smoother_gains, smoother_offsets, smoother_covs):
    own_gain = smoother_gains[0]
    own_cov = smoother_covs[0]
    rows, size = own_cov.shape
    start = lax.axis_index("rows") * rows
    vmem = pl.BlockSpec(memory_space=pltpu.VMEM)
    hbm = pl.BlockSpec(memory_space=pltpu.HBM)
    gathers = 3 if steps == 4 else 4
    half = size // 2
    unit = unit_rows(rows)
    per = rows // unit
    chunks = unit // CHUNK
    tiles = half // LANES
    units = half // unit
    upt = LANES // unit
    slots = 2 if steps == 4 else 3
    bf16 = jnp.bfloat16
    dma = pltpu.SemaphoreType.DMA
    both = pl.pallas_call(
        functools.partial(kernel, steps, n),
        out_shape=jax.ShapeDtypeStruct((rows + PAD, size), bf16),
        in_specs=[hbm, hbm, hbm],
        out_specs=vmem,
        scratch_shapes=[
            pltpu.VMEM((gathers, half, size), bf16),
            pltpu.VMEM((gathers + 1, rows + PAD, size), bf16),
            pltpu.VMEM((gathers, rows, half), bf16),
            pltpu.VMEM((gathers, units) + folded(rows), bf16),
            pltpu.VMEM((gathers, n, per) + folded(rows), bf16),
            pltpu.VMEM((rows + PAD, size), bf16),
            pltpu.VMEM((n, 4, 1, rows), bf16),
            pltpu.VMEM((4, 1, size), jnp.float32),
            dma((slots, 2)),
            dma((slots, units, chunks)),
            dma((slots,)),
            dma((gathers,)),
            dma((1,)),
            dma((2,)),
            dma((gathers,)),
            dma((2,)),
            dma((1,)),
            dma((2,)),
            dma((2,)),
            dma((1,)),
            dma((1,)),
            dma((gathers,)),
            dma((2, n)),
            dma((2, n)),
            dma((gathers,)),
            dma((gathers,)),
            dma((gathers,)),
            dma((2,)),
            dma((2,)),
            dma((2,)),
            dma((1,)),
        ],
        compiler_params=pltpu.CompilerParams(
            collective_id=0, has_side_effects=True, vmem_limit_bytes=40 << 20
        ),
    )(pltpu.with_memory_space_constraint(own_gain, pltpu.HBM), pltpu.with_memory_space_constraint(smoother_offsets, pltpu.HBM), pltpu.with_memory_space_constraint(own_cov, pltpu.HBM))
    mean = lax.dynamic_slice(both, (rows, start), (1, rows))
    return mean, both[None, :rows]


def solution(mesh):
    in_specs = (P("tm", "rows", None), P("tm", "rows"), P("tm", "rows", None))
    out_specs = (P("tm", "rows"), P("tm", "rows", None))
    body = functools.partial(shards, mesh.shape["tm"], mesh.shape["rows"])
    return jax.shard_map(body, mesh=mesh, in_specs=in_specs, out_specs=out_specs, check_vma=False)
```

```python
import functools
import math

import jax
import jax.numpy as jnp
from jax import lax
from jax.experimental import pallas as pl
from jax.experimental.pallas import tpu as pltpu
from jax.sharding import PartitionSpec as P

MESH = pl.DeviceIdType.MESH
LANES = 128
PAD = 16
CHUNK = 32
GAIN_AT = 2
TOP_AT = 1
BUNDLE_AT = 2
BEHIND = 3
LEFT_PARTS = 3
TILES_AT_ONCE = 2
CONTRACT_LAST = (((1,), (1,)), ((), ()))


def unit_rows(rows):
    return math.gcd(rows, LANES)


def share_sizes(rows, n):
    unit = unit_rows(rows)
    per, upt = rows // unit, LANES // unit
    planes = [[(per * d + i) // upt % 2 for i in range(per)] for d in range(n)]
    return sorted({row.count(x) for row in planes for x in range(2)} - {0})


def line_totals(rows, n):
    unit = unit_rows(rows)
    per, upt, spots = rows // unit, LANES // unit, n // 2
    beside, ahead = set(), set()
    for x in range(2):
        for lane in range(2):
            along = [
                sum((per * (at * 2 + lane) + i) // upt % 2 == x for i in range(per))
                for at in range(spots)
            ]
            beside.add(sum(along))
            for spot in range(spots):
                ahead.add(
                    (sum(along[:spot + 1]) if spot < spots - 1 else 0)
                    + (sum(along[spot:]) if spot > 0 else 0)
                )
    return sorted(beside), sorted(ahead)


def folded(rows):
    unit = unit_rows(rows)
    return (unit + unit // 2, LANES) if rows == 192 else (unit, rows)


def kernel(
    steps, n, gain_in, offset_in, cov_hbm, out,
    e_half, cov, l_in, left_out, left_in, left, gbuf, gsum,
    line_send, line_recv, pass_send, full_recv, init_send,
    l_send, l_recv, top_sems, load_sems, g_send, g_recv, gb_send, gb_recv,
    left_send, left_recv, across_recv, fwd_send, x_send, x_recv, out_sems, mid_sems,
    low_send, low_recv,
):
    t = lax.axis_index("tm")
    r = lax.axis_index("rows")
    spot, lane, spots = r // 2, r % 2, n // 2
    quads = steps // 4
    gathers = e_half.shape[0]
    q = t // 4
    b = q * 4
    j_own = t % 4
    p = j_own // 2
    core = t % 2
    top = q == quads - 1
    partner = b + 2 * (1 - p) + 1
    size = gain_in.shape[1]
    rows = size // n
    half = size // 2
    unit = unit_rows(rows)
    per = rows // unit
    upt = LANES // unit
    tiles = half // LANES
    units = half // unit
    chunks = unit // CHUNK
    picks = upt // 2
    counts = share_sizes(rows, n)

    def aligned(x, m):
        return pl.multiple_of(x, m)

    def remote(src, dst, send, recv, device):
        return pltpu.make_async_remote_copy(
            src_ref=src, dst_ref=dst, send_sem=send, recv_sem=recv,
            device_id=device, device_id_type=MESH,
        )

    def plane_of(d, i):
        return ((per * d + i) // upt) % 2

    def place_of(d, i):
        u = per * d + i
        return (u // upt // 2) * upt + u % upt

    def pick(o, w, k):
        start = per * o
        i = (upt * p + 2 * k + w - start + 2 * upt * n) % (2 * upt)
        return i

    mine = [plane_of(r, i) for i in range(per)]
    held = sum([1 - (x + p) % 2 for x in mine])
    first_held = (1 - (mine[0] + p) % 2) * 0 + ((mine[0] + p) % 2) * (per - held)
    first_other = (1 - (mine[0] + p) % 2) * held

    def owner(v):
        u = ((v // upt) * 2 + p) * upt + v % upt
        return u // per, u % per

    def unit_span(v, c, length):
        return pl.ds(aligned(v * unit + c * CHUNK, CHUNK), length)

    def nat_columns(tile, plane):
        return pl.ds(aligned((tile * 2 + plane) * LANES, LANES), LANES)

    def half_columns(tile):
        return pl.ds(aligned(tile * LANES, LANES), LANES)

    def other_row(i):
        return (r + i) % n

    barrier = pltpu.get_barrier_semaphore()

    def greet(tt, rr):
        pl.semaphore_signal(barrier, inc=1, device_id=(tt, rr), device_id_type=MESH)

    for i in range(1, 4):
        greet(b + (j_own + i) % 4, r)
    @pl.when(core == 1)
    def _():
        def greet_row(i, carry):
            greet(t, other_row(i))
            return carry

        lax.fori_loop(1, n, greet_row, 0)

    @pl.when(core == 0)
    def _():
        greet(t, spot * 2 + 1 - lane)
        greet(t + 1, spot * 2 + 1 - lane)

        @pl.when(spot > 0)
        def _():
            greet(t, r - 2)

        @pl.when(spot < spots - 1)
        def _():
            greet(t, r + 2)

    @pl.when(core == 1)
    def _():
        greet(t - 1, spot * 2 + 1 - lane)

    inner = (spot + spots - 1) // spots + (2 * spots - 2 - spot) // spots
    greetings = 3 + core * n + (1 - core) * (2 + inner)
    if quads > 1:
        for step in (-4, 4):
            near = (q * 4 + step >= 0) & (q * 4 + step < steps)

            @pl.when((core == 1) & near)
            def _():
                for i in (1, 3):
                    greet(b + step + i, r)

        greetings = greetings + core * 2 * (((q + quads - 1) // quads) + (2 * quads - 2 - q) // quads * 1)

    @pl.when(j_own == 3)
    def _():
        pltpu.make_async_copy(cov_hbm, cov.at[3, pl.ds(0, rows), :], load_sems.at[0]).start()

    pl.semaphore_wait(barrier, greetings)

    def slot_of(j):
        return 0 if j == 2 else (2 if j == 3 else j)

    def source(j, what):
        for i in range(per):
            x, v = plane_of(r, i), place_of(r, i)
            to = b + 2 * x + (1 if j == 2 else 0)
            for c in range(chunks):
                src = gain_in.at[pl.ds(i * unit + c * CHUNK, CHUNK), :]
                dst = e_half.at[j, unit_span(v, c, CHUNK), :]
                recv = line_recv.at[slot_of(j), v, c]

                def go():
                    remote(src, dst, init_send.at[0], recv, (to, r)).start()

                if j == 0:
                    @pl.when(to == t)
                    def _():
                        pltpu.make_async_copy(src, dst, recv).start()

                    pl.when(to != t)(go)
                else:
                    go()

    def source_gone(j):
        for count in ([per] if j else counts + [0]):
            @pl.when((per - held == count) | (j != 0))
            def _():
                if count:
                    block = gain_in.at[pl.ds(0, count * unit), :]
                    remote(
                        block, e_half.at[j, pl.ds(0, count * unit), :], init_send.at[0],
                        line_recv.at[0, 0, 0], (partner, r),
                    ).wait_send()

    def whole_arrival(j):
        return remote(e_half.at[j], e_half.at[j], init_send.at[0], full_recv.at[j], (t - 1, r))

    def unit_of(j, v):
        return e_half.at[j, unit_span(v, 0, unit), :]

    def line_units(d, act):
        for stream in range(2):
            at = spot - d if stream == 0 else spot + d
            inside = (at >= 0) & (at < spots)
            o = jnp.where(inside, at * 2 + lane, r)
            for w in range(2):
                for k in range(picks):
                    i = pick(o, w, k)
                    act(stream, inside & (i < per), place_of(o, i), w * picks + k)

    def onward(stream):
        return (spot < spots - 1) if stream == 0 else (spot > 0)

    def line_hop(j, d, with_pass):
        slot = slot_of(j)

        def forward(stream, c, v, which):
            span = unit_span(v, c, CHUNK)
            block = e_half.at[j, span, :]

            @pl.when(onward(stream))
            def _():
                remote(
                    block, block, line_send.at[slot, 0],
                    line_recv.at[slot, v, c], (t, r + 2 if stream == 0 else r - 2),
                ).start()

        def aside(stream, c, v, which):
            block = e_half.at[j, unit_span(v, c, CHUNK), :]
            if with_pass:
                remote(
                    block, block, line_send.at[slot, 1], full_recv.at[j],
                    (t + 1, spot * 2 + 1 - lane),
                ).start()
                if c == chunks - 1:
                    block = unit_of(j, v)
                    remote(
                        block, block, pass_send.at[slot], full_recv.at[j],
                        (t + 1, r),
                    ).start()
            else:
                remote(
                    block, block, line_send.at[slot, 1],
                    line_recv.at[slot, v, c], (t, spot * 2 + 1 - lane),
                ).start()

        for c in range(chunks):
            if isinstance(d, int):
                for w in range(2):
                    for k in range(picks):
                        i = pick(r, w, k)
                        v = place_of(r, i)
                        which = w * picks + k

                        @pl.when(i < per)
                        def _():
                            unit_chunk(j, v, c).wait_recv()
                            forward(0, c, v, which)
                            forward(1, c, v, which)
                            aside(0, c, v, which)
            else:
                def act(stream, ok, v, which):
                    @pl.when(ok)
                    def _():
                        unit_chunk(j, v, c).wait_recv()
                        forward(stream, c, v, which)
                        aside(stream, c, v, which)

                line_units(d, act)

    def unit_chunk(j, v, c):
        block = e_half.at[j, unit_span(v, c, CHUNK), :]
        return remote(
            block, block, init_send.at[0], line_recv.at[slot_of(j), v, c], (partner, r)
        )

    def line_gone(j, with_pass):
        slot = slot_of(j)
        along = [
            sum([1 - (plane_of(at * 2 + lane, i) + p) % 2 for i in range(per)])
            for at in range(spots)
        ]
        beside = sum(along)
        ahead = 0
        for at in range(spots):
            ahead = ahead + along[at] * jnp.where((at <= spot) & (spot < spots - 1), 1, 0)
            ahead = ahead + along[at] * jnp.where((at >= spot) & (spot > 0), 1, 0)

        def sent(count, total, sem):
            @pl.when(count == total)
            def _():
                block = e_half.at[j, pl.ds(0, total * unit), :]
                remote(block, block, sem, line_recv.at[0, 0, 0], (partner, r)).wait_send()

        for total in line_totals(rows, n)[0]:
            sent(beside, total, line_send.at[slot, 1])
            if with_pass:
                sent(beside, total, pass_send.at[slot])
        for total in line_totals(rows, n)[1]:
            sent(ahead, total, line_send.at[slot, 0])

    def l_copy(j, plane, tile):
        return remote(
            cov_hbm.at[:, nat_columns(tile, plane)],
            l_in.at[j, :, half_columns(tile)],
            l_send.at[plane], l_recv.at[j], (b + 2 * plane + 1, r),
        )

    def l_local(j, tile):
        return pltpu.make_async_copy(
            cov_hbm.at[:, nat_columns(tile, p)], l_in.at[j, :, half_columns(tile)],
            l_recv.at[j],
        )

    def l_whole(j, plane):
        return remote(
            l_in.at[j], l_in.at[j], l_send.at[plane], l_recv.at[j], (partner, r)
        )

    def top_copy():
        return remote(
            cov_hbm, cov.at[3, pl.ds(0, rows), :], top_sems.at[0], top_sems.at[1], (t - 2 * (2 * p - 1), r)
        )

    def g_copy(plane):
        return remote(
            offset_in, gbuf.at[r, j_own], g_send.at[plane], g_recv.at[0], (b + 2 * plane + 1, r)
        )

    def g_bundle(o, source):
        return remote(gbuf.at[source], gbuf.at[source], gb_send.at[0], gb_recv.at[0], (t, o))

    def left_copy(j, d, i, v):
        return remote(
            left_out.at[j, v], left_in.at[j, r, i], left_send.at[j], left_recv.at[j % 2, r], (t, d)
        )

    def left_across(j, v, i):
        return remote(
            left_out.at[j, v], left_in.at[j, r, i], left_send.at[j], across_recv.at[j % 2, r],
            (partner, r),
        )

    def left_block(j, o, start, count, recv):
        block = left_in.at[j, o, pl.ds(start, count)]
        return remote(block, block, fwd_send.at[j], recv, (partner, r))

    def left_sent(j):
        remote(
            left_out.at[j], left_out.at[j], left_send.at[j], left_recv.at[j % 2, r], (partner, r)
        ).wait_send()

    def left_pass(j, o, count):
        return left_block(j, o, first_held, count, across_recv.at[j % 2, o])

    def pass_sent(j, count):
        block = left_in.at[j, pl.ds(0, n - 1), pl.ds(0, count)]
        remote(block, block, fwd_send.at[j], across_recv.at[j % 2, r], (partner, r)).wait_send()

    def x_copy(j, tile, plane):
        columns = nat_columns(tile, plane)
        return remote(
            cov.at[j, :, columns], cov.at[j, :, columns], x_send.at[j], x_recv.at[j],
            (partner, r),
        )

    def x_whole(j):
        block = cov.at[j, :, pl.ds(0, half)]
        return remote(block, block, x_send.at[j], x_recv.at[j], (partner, r))

    def out_copy(tile, plane):
        columns = nat_columns(tile, plane)
        return remote(
            cov.at[0, :, columns], out.at[:, columns], out_sems.at[0], out_sems.at[1], (b, r),
        )

    def out_arrival():
        return remote(cov.at[0], out, out_sems.at[0], out_sems.at[1], (t + 1, r))

    def out_gone():
        block = cov.at[0, :, pl.ds(0, half)]
        remote(block, out.at[:, pl.ds(0, half)], out_sems.at[0], out_sems.at[1], (b, r)).wait_send()

    def mid_copy():
        return remote(cov.at[2], out, mid_sems.at[0], mid_sems.at[1], (b + 2, r))

    def low_copy(tile, plane, dest):
        columns = nat_columns(tile, plane)
        return remote(
            cov.at[0, :, columns], cov.at[gathers, :, columns], low_send.at[dest],
            low_recv.at[0], (b - 4 + 2 * dest + 1, r),
        )

    def both(copies, what):
        for copy in copies:
            getattr(copy, what)()

    def send_l(j):
        for plane in range(2):
            for tile in range(tiles):
                @pl.when(b + 2 * plane + 1 != t)
                def _():
                    l_copy(j, plane, tile).start()

                @pl.when(b + 2 * plane + 1 == t)
                def _():
                    l_local(j, tile).start()

    def l_gone(j):
        for plane in range(2):
            @pl.when(b + 2 * plane + 1 != t)
            def _():
                l_whole(j, plane).wait_send()

    def send_g():
        for plane in range(2):
            @pl.when(b + 2 * plane + 1 != t)
            def _():
                g_copy(plane).start()

    def g_gone():
        for plane in range(2):
            @pl.when(b + 2 * plane + 1 != t)
            def _():
                g_copy(plane).wait_send()

    @pl.when(core == 0)
    def _mover():
        @pl.when(j_own == 2)
        def _():
            source(2, "start")
            send_g()
            send_l(2)

        @pl.when(j_own == 0)
        def _():
            send_g()
            source(0, "start")
            send_l(0)

        if quads > 1:
            @pl.when(q < quads - 1)
            def _():
                line_hop(3, 0, True)

                def hop3(d, carry):
                    line_hop(3, d, True)
                    return carry

                lax.fori_loop(1, spots, hop3, 0)

        line_hop(1, 0, True)

        def hop_step(d, carry):
            @pl.when(d < spots)
            def _():
                line_hop(1, d, True)

            @pl.when(d == BEHIND)
            def _():
                line_hop(0, 0, True)

            @pl.when(d > BEHIND)
            def _():
                line_hop(0, d - BEHIND, True)

            return carry

        lax.fori_loop(1, spots + BEHIND, hop_step, 0)

        if quads > 1:
            @pl.when(q < quads - 1)
            def _():
                line_gone(3, True)

        line_gone(1, True)
        line_gone(0, True)

        @pl.when(j_own == 2)
        def _():
            source_gone(2)
            l_gone(2)

        @pl.when(j_own == 0)
        def _():
            source_gone(0)
            l_gone(0)

        g_gone()

        @pl.when(j_own == 2)
        def _():
            mid_copy().wait_recv()

        @pl.when(j_own == 0)
        def _():
            out_arrival().wait_recv()

    @pl.when(core == 1)
    def _worker():
        send_g()

        pltpu.make_async_copy(offset_in, gbuf.at[r, j_own], g_recv.at[1]).start()

        def store_left(j, v, block):
            if rows == 192:
                left_out[j, v, 0:unit, :] = block[:, :LANES]
                for s in range(2):
                    left_out[j, v, unit:, s * 64:(s + 1) * 64] = block[
                        s * unit // 2:(s + 1) * unit // 2, LANES:
                    ]
            else:
                left_out[j, v] = block

        def place_left(j, d, i):
            at, low = d * rows, i * unit
            if rows == 192:
                left[low:low + unit, at:at + LANES] = left_in[j, d, i, 0:unit, :]
                for s in range(2):
                    left[low + s * unit // 2:low + (s + 1) * unit // 2, at + LANES:at + rows] = (
                        left_in[j, d, i, unit:, s * 64:(s + 1) * 64]
                    )
            else:
                left[low:low + unit, at:at + rows] = left_in[j, d, i]

        def send_left(j, v, d, i):
            @pl.when(d != r)
            def _():
                left_copy(j, d, i, v).start()

            @pl.when(d == r)
            def _():
                left_across(j, v, i).start()
                left_in[j, r, i] = left_out[j, v]

        def left_unit(o, i):
            v = place_of(o, i)
            product = lax.dot_general(
                e_half[2, unit_span(v, 0, unit), :], cov[3, 0:rows, :], CONTRACT_LAST,
                preferred_element_type=jnp.float32,
            )
            store_left(2, v, product.astype(jnp.bfloat16))
            send_left(2, v, o, i)

        def later(d):
            @pl.when((d == TOP_AT) & (j_own == 3) & top)
            def _():
                top_copy().start()

            @pl.when((d == 1) & (j_own == 1))
            def _():
                send_l(1)

            @pl.when(d == GAIN_AT)
            def _():
                @pl.when(j_own == 1)
                def _():
                    source(1, "start")

                if quads > 1:
                    @pl.when((j_own == 3) & jnp.logical_not(top))
                    def _():
                        source(3, "start")
                        send_l(3)

            @pl.when(d == BUNDLE_AT)
            def _():
                remote(
                    gbuf.at[r, pl.ds(0, 3)], gbuf.at[r, pl.ds(0, 3)], g_send.at[0], g_recv.at[0],
                    (partner, r),
                ).wait_recv()

                pltpu.make_async_copy(offset_in, gbuf.at[r, j_own], g_recv.at[1]).wait()

                def bundle(i, c):
                    g_bundle(other_row(i), r).start()
                    return c

                lax.fori_loop(1, n, bundle, 0)

        line_hop(2, 0, False)

        def e2_hop(d, carry):
            line_hop(2, d, False)
            later(d)
            return carry

        lax.fori_loop(1, spots, e2_hop, 0)

        @pl.when(top)
        def _():
            @pl.when(j_own == 1)
            def _():
                top_copy().wait_recv()

            @pl.when(j_own == 3)
            def _():
                pltpu.make_async_copy(
                    cov_hbm, cov.at[3, pl.ds(0, rows), :], load_sems.at[0]
                ).wait()

            def own_lane(at, carry):
                for i in range(per):
                    @pl.when(plane_of(at * 2 + lane, i) == p)
                    def _():
                        left_unit(at * 2 + lane, i)
                return carry

            lax.fori_loop(0, spots, own_lane, 0)

        def other_lane(d, carry):
            for side in range(2):
                at = spot - d if side == 0 else spot + d
                o = at * 2 + 1 - lane
                for i in range(per):
                    @pl.when(
                        (at >= 0) & (at < spots) & ((side == 0) | (d > 0))
                        & (plane_of(o, i) == p)
                    )
                    def _():
                        for c in range(chunks):
                            unit_chunk(2, place_of(o, i), c).wait_recv()

                        @pl.when(top)
                        def _():
                            left_unit(o, i)
            return carry

        lax.fori_loop(0, spots, other_lane, 0)

        def bundles():
            return remote(
                gbuf.at[pl.ds(0, n - 1)], gbuf.at[pl.ds(0, n - 1)], gb_send.at[0], gb_recv.at[0],
                (partner, r),
            )

        bundles().wait_recv()
        for i in range(n):
            gsum[:, :, i * rows:(i + 1) * rows] = gbuf[i].astype(jnp.float32)

        @pl.when(top)
        def _():
            cov[3, rows:, :] = jnp.broadcast_to(gsum[3], (PAD, size)).astype(jnp.bfloat16)

        first_step = jnp.where(top, 2, 3) if quads > 1 else 2
        started = jnp.where(top, 1, 0)

        def chain(k, carry):
            j = first_step - k

            if quads > 1:
                @pl.when(jnp.logical_not(top) & (j == 3))
                def _():
                    remote(
                        cov.at[0], cov.at[gathers], low_send.at[0], low_recv.at[0], (partner, r)
                    ).wait_recv()

            @pl.when(k >= started)
            def _():
                @pl.when(j != 2)
                def _():
                    whole_arrival(j).wait_recv()

                share = units // LEFT_PARTS

                def left_part(g, c):
                    span = pl.ds(aligned(g * share * unit, share * unit), share * unit)
                    product = lax.dot_general(
                        e_half[j, span, :], cov[j + 1, 0:rows, :], CONTRACT_LAST,
                        preferred_element_type=jnp.float32,
                    ).astype(jnp.bfloat16)
                    for i in range(share):
                        store_left(j, g * share + i, product[i * unit:(i + 1) * unit])

                    def send(i, cc):
                        v = g * share + i
                        d, at = owner(v)
                        send_left(j, v, d, at)
                        return cc

                    lax.fori_loop(0, share, send, 0)
                    return c

                lax.fori_loop(0, LEFT_PARTS, left_part, 0)

            for count in counts:
                @pl.when(held == count)
                def _():
                    def pass_on(i, c):
                        o = other_row(i)
                        left_block(j, o, first_held, count, left_recv.at[j % 2, o]).wait_recv()
                        left_pass(j, o, count).start()
                        return c

                    lax.fori_loop(1, n, pass_on, 0)

            for count in counts:
                @pl.when(per - held == count)
                def _():
                    def take(i, c):
                        left_block(j, i, first_other, count, across_recv.at[j % 2, i]).wait_recv()
                        return c

                    lax.fori_loop(0, n, take, 0)

            for d in range(n):
                for at in range(per):
                    place_left(j, d, at)
            left[rows:, :] = cov[j + 1, rows:, :]

            l_whole(j, 0).wait_recv()

            def right_part(g, c):
                wide = TILES_AT_ONCE * LANES
                product = lax.dot_general(
                    left[...], e_half[j, pl.ds(aligned(g * wide, wide), wide), :], CONTRACT_LAST,
                    preferred_element_type=jnp.float32,
                )
                for s in range(TILES_AT_ONCE):
                    tile = g * TILES_AT_ONCE + s
                    columns = nat_columns(tile, p)
                    block = product[:, s * LANES:(s + 1) * LANES]
                    cov[j, 0:rows, columns] = (
                        block[:rows] + l_in[j, :, half_columns(tile)].astype(jnp.float32)
                    ).astype(jnp.bfloat16)
                    cov[j, rows:, columns] = (
                        block[rows:] + gsum[j, :, columns]
                    ).astype(jnp.bfloat16)

                    @pl.when(j > 0)
                    def _():
                        x_copy(j, tile, p).start()

                    @pl.when(j == 0)
                    def _():
                        out_copy(tile, p).start()
                        if quads > 1:
                            @pl.when(q > 0)
                            def _():
                                for dest in range(2):
                                    low_copy(tile, p, dest).start()
                return c

            lax.fori_loop(0, tiles // TILES_AT_ONCE, right_part, 0)

            @pl.when(j > 0)
            def _():
                x_whole(j).wait_recv()

            @pl.when((j == 2) & (j_own == 3))
            def _():
                mid_copy().start()

            return carry

        lax.fori_loop(0, first_step + 1, chain, 0)

        out[...] = cov[j_own]

        def sent(k, carry):
            j = first_step - k

            left_sent(j)
            for count in counts:
                @pl.when(held == count)
                def _():
                    pass_sent(j, count)

            @pl.when(j > 0)
            def _():
                x_whole(j).wait_send()

            return carry

        lax.fori_loop(0, first_step + 1, sent, 0)

        line_gone(2, False)
        bundles().wait_send()
        out_gone()
        if quads > 1:
            @pl.when(q > 0)
            def _():
                for dest in range(2):
                    remote(
                        cov.at[0, :, pl.ds(0, half)], cov.at[gathers, :, pl.ds(0, half)],
                        low_send.at[dest], low_recv.at[0], (partner, r),
                    ).wait_send()
        g_gone()

        @pl.when(j_own == 1)
        def _():
            source_gone(1)
            l_gone(1)

        if quads > 1:
            @pl.when((j_own == 3) & jnp.logical_not(top))
            def _():
                source_gone(3)
                l_gone(3)

        @pl.when((j_own == 3) & top)
        def _():
            top_copy().wait_send()

        @pl.when(j_own == 3)
        def _():
            mid_copy().wait_send()


def shards(steps, n, smoother_gains, smoother_offsets, smoother_covs):
    own_gain = smoother_gains[0]
    own_cov = smoother_covs[0]
    rows, size = own_cov.shape
    start = lax.axis_index("rows") * rows
    vmem = pl.BlockSpec(memory_space=pltpu.VMEM)
    hbm = pl.BlockSpec(memory_space=pltpu.HBM)
    gathers = 3 if steps == 4 else 4
    half = size // 2
    unit = unit_rows(rows)
    per = rows // unit
    chunks = unit // CHUNK
    tiles = half // LANES
    units = half // unit
    upt = LANES // unit
    slots = 2 if steps == 4 else 3
    bf16 = jnp.bfloat16
    dma = pltpu.SemaphoreType.DMA
    both = pl.pallas_call(
        functools.partial(kernel, steps, n),
        out_shape=jax.ShapeDtypeStruct((rows + PAD, size), bf16),
        in_specs=[hbm, hbm, hbm],
        out_specs=vmem,
        scratch_shapes=[
            pltpu.VMEM((gathers, half, size), bf16),
            pltpu.VMEM((gathers + 1, rows + PAD, size), bf16),
            pltpu.VMEM((gathers, rows, half), bf16),
            pltpu.VMEM((gathers, units) + folded(rows), bf16),
            pltpu.VMEM((gathers, n, per) + folded(rows), bf16),
            pltpu.VMEM((rows + PAD, size), bf16),
            pltpu.VMEM((n, 4, 1, rows), bf16),
            pltpu.VMEM((4, 1, size), jnp.float32),
            dma((slots, 2)),
            dma((slots, units, chunks)),
            dma((slots,)),
            dma((gathers,)),
            dma((1,)),
            dma((2,)),
            dma((gathers,)),
            dma((2,)),
            dma((1,)),
            dma((2,)),
            dma((2,)),
            dma((1,)),
            dma((1,)),
            dma((gathers,)),
            dma((2, n)),
            dma((2, n)),
            dma((gathers,)),
            dma((gathers,)),
            dma((gathers,)),
            dma((2,)),
            dma((2,)),
            dma((2,)),
            dma((1,)),
        ],
        compiler_params=pltpu.CompilerParams(
            collective_id=0, has_side_effects=True, vmem_limit_bytes=40 << 20
        ),
    )(pltpu.with_memory_space_constraint(own_gain, pltpu.HBM), pltpu.with_memory_space_constraint(smoother_offsets, pltpu.HBM), pltpu.with_memory_space_constraint(own_cov, pltpu.HBM))
    mean = lax.dynamic_slice(both, (rows, start), (1, rows))
    return mean, both[None, :rows]


def solution(mesh):
    in_specs = (P("tm", "rows", None), P("tm", "rows"), P("tm", "rows", None))
    out_specs = (P("tm", "rows"), P("tm", "rows", None))
    body = functools.partial(shards, mesh.shape["tm"], mesh.shape["rows"])
    return jax.shard_map(body, mesh=mesh, in_specs=in_specs, out_specs=out_specs, check_vma=False)
```

```python
import functools
import math

import jax
import jax.numpy as jnp
from jax import lax
from jax.experimental import pallas as pl
from jax.experimental.pallas import tpu as pltpu
from jax.sharding import PartitionSpec as P

MESH = pl.DeviceIdType.MESH
LANES = 128
PAD = 16
CHUNK = 32
GAIN_AT = 2
TOP_AT = 1
BUNDLE_AT = 3
BEHIND = 3
SPREAD_AT = 1
LEFT_PARTS = 2
TILES_AT_ONCE = 2
CONTRACT_LAST = (((1,), (1,)), ((), ()))


def unit_rows(rows):
    return math.gcd(rows, LANES)


def share_sizes(rows, n):
    unit = unit_rows(rows)
    per, upt = rows // unit, LANES // unit
    planes = [[(per * d + i) // upt % 2 for i in range(per)] for d in range(n)]
    return sorted({row.count(x) for row in planes for x in range(2)})


def line_totals(rows, n):
    unit = unit_rows(rows)
    per, upt, spots = rows // unit, LANES // unit, n // 2
    beside, ahead = set(), set()
    for x in range(2):
        for lane in range(2):
            along = [
                sum((per * (at * 2 + lane) + i) // upt % 2 == x for i in range(per))
                for at in range(spots)
            ]
            beside.add(sum(along))
            for spot in range(spots):
                ahead.add(
                    (sum(along[:spot + 1]) if spot < spots - 1 else 0)
                    + (sum(along[spot:]) if spot > 0 else 0)
                )
    return sorted(beside), sorted(ahead)


def folded(rows):
    unit = unit_rows(rows)
    return (unit + unit // 2, LANES) if rows == 192 else (unit, rows)


def kernel(
    steps, n, gain_in, offset_in, cov_hbm, out,
    e_half, cov, l_in, left_out, left_in, left, gbuf, gsum,
    line_send, line_recv, pass_send, full_recv, init_send,
    l_send, l_recv, top_sems, load_sems, g_send, g_recv, gb_send, gb_recv,
    left_send, left_recv, across_recv, fwd_send, x_send, x_recv, out_sems, mid_sems,
    low_send, low_recv,
):
    t = lax.axis_index("tm")
    r = lax.axis_index("rows")
    spot, lane, spots = r // 2, r % 2, n // 2
    quads = steps // 4
    gathers = e_half.shape[0]
    q = t // 4
    b = q * 4
    j_own = t % 4
    p = j_own // 2
    core = t % 2
    top = q == quads - 1
    partner = b + 2 * (1 - p) + 1
    size = gain_in.shape[1]
    rows = size // n
    half = size // 2
    unit = unit_rows(rows)
    per = rows // unit
    upt = LANES // unit
    tiles = half // LANES
    units = half // unit
    chunks = unit // CHUNK
    picks = upt // 2
    sizes = share_sizes(rows, n)
    counts = [size for size in sizes if size]
    greet_all = 0 in sizes

    def aligned(x, m):
        return pl.multiple_of(x, m)

    def remote(src, dst, send, recv, device):
        return pltpu.make_async_remote_copy(
            src_ref=src, dst_ref=dst, send_sem=send, recv_sem=recv,
            device_id=device, device_id_type=MESH,
        )

    def plane_of(d, i):
        return ((per * d + i) // upt) % 2

    def place_of(d, i):
        u = per * d + i
        return (u // upt // 2) * upt + u % upt

    def pick(o, w, k):
        start = per * o
        i = (upt * p + 2 * k + w - start + 2 * upt * n) % (2 * upt)
        return i

    mine = [plane_of(r, i) for i in range(per)]
    held = sum([1 - (x + p) % 2 for x in mine])
    first_held = (1 - (mine[0] + p) % 2) * 0 + ((mine[0] + p) % 2) * (per - held)
    first_other = (1 - (mine[0] + p) % 2) * held

    def owner(v):
        u = ((v // upt) * 2 + p) * upt + v % upt
        return u // per, u % per

    def unit_span(v, c, length):
        return pl.ds(aligned(v * unit + c * CHUNK, CHUNK), length)

    def nat_columns(tile, plane):
        return pl.ds(aligned((tile * 2 + plane) * LANES, LANES), LANES)

    def half_columns(tile):
        return pl.ds(aligned(tile * LANES, LANES), LANES)

    def other_row(i):
        return (r + i) % n

    barrier = pltpu.get_barrier_semaphore()

    def greet(tt, rr):
        pl.semaphore_signal(barrier, inc=1, device_id=(tt, rr), device_id_type=MESH)

    for i in range(1, 4):
        greet(b + (j_own + i) % 4, r)
    greet(t, spot * 2 + 1 - lane)
    greet(t + 1 - 2 * core, spot * 2 + 1 - lane)

    @pl.when(spot > 0)
    def _():
        greet(t, r - 2)

    @pl.when(spot < spots - 1)
    def _():
        greet(t, r + 2)

    inner = (spot + spots - 1) // spots + (2 * spots - 2 - spot) // spots
    greetings = 5 + inner
    if greet_all:
        @pl.when(core == 1)
        def _():
            def greet_row(i, carry):
                o = other_row(i)
                near = (o // 2 == spot) | ((o % 2 == lane) & (o // 2 - spot < 2) & (spot - o // 2 < 2))

                @pl.when(jnp.logical_not(near))
                def _():
                    greet(t, o)
                return carry

            lax.fori_loop(1, n, greet_row, 0)

        greetings = greetings + core * (n - 2 - inner)
    if quads > 1:
        for step in (-4, 4):
            near = (q * 4 + step >= 0) & (q * 4 + step < steps)

            @pl.when((core == 1) & near)
            def _():
                for i in (1, 3):
                    greet(b + step + i, r)

        greetings = greetings + core * 2 * (((q + quads - 1) // quads) + (2 * quads - 2 - q) // quads * 1)

    @pl.when(j_own == 3)
    def _():
        pltpu.make_async_copy(cov_hbm, cov.at[3, pl.ds(0, rows), :], load_sems.at[0]).start()

    pl.semaphore_wait(barrier, greetings)

    def slot_of(j):
        return 0 if j == 2 else (2 if j == 3 else j)

    def source(j, what):
        for i in range(per):
            x, v = plane_of(r, i), place_of(r, i)
            to = b + 2 * x + (1 if j == 2 else 0)
            for c in range(chunks):
                src = gain_in.at[pl.ds(i * unit + c * CHUNK, CHUNK), :]
                dst = e_half.at[j, unit_span(v, c, CHUNK), :]
                recv = line_recv.at[slot_of(j), v, c]

                def go():
                    remote(src, dst, init_send.at[0], recv, (to, r)).start()

                if j == 0:
                    @pl.when(to == t)
                    def _():
                        pltpu.make_async_copy(src, dst, recv).start()

                    pl.when(to != t)(go)
                else:
                    go()

    def source_gone(j):
        for count in ([per] if j else counts + [0]):
            @pl.when((per - held == count) | (j != 0))
            def _():
                if count:
                    block = gain_in.at[pl.ds(0, count * unit), :]
                    remote(
                        block, e_half.at[j, pl.ds(0, count * unit), :], init_send.at[0],
                        line_recv.at[0, 0, 0], (partner, r),
                    ).wait_send()

    def whole_arrival(j):
        return remote(e_half.at[j], e_half.at[j], init_send.at[0], full_recv.at[j], (t - 1, r))

    def unit_of(j, v):
        return e_half.at[j, unit_span(v, 0, unit), :]

    def line_units(d, act):
        for stream in range(2):
            at = spot - d if stream == 0 else spot + d
            inside = (at >= 0) & (at < spots)
            o = jnp.where(inside, at * 2 + lane, r)
            for w in range(2):
                for k in range(picks):
                    i = pick(o, w, k)
                    act(stream, inside & (i < per), place_of(o, i), w * picks + k)

    def onward(stream):
        return (spot < spots - 1) if stream == 0 else (spot > 0)

    def line_hop(j, d, with_pass):
        slot = slot_of(j)

        def forward(stream, c, v, which):
            span = unit_span(v, c, CHUNK)
            block = e_half.at[j, span, :]

            @pl.when(onward(stream))
            def _():
                remote(
                    block, block, line_send.at[slot, 0],
                    line_recv.at[slot, v, c], (t, r + 2 if stream == 0 else r - 2),
                ).start()

        def aside(stream, c, v, which):
            block = e_half.at[j, unit_span(v, c, CHUNK), :]
            if with_pass:
                remote(
                    block, block, line_send.at[slot, 1], full_recv.at[j],
                    (t + 1, spot * 2 + 1 - lane),
                ).start()
                if c == chunks - 1:
                    block = unit_of(j, v)
                    remote(
                        block, block, pass_send.at[slot], full_recv.at[j],
                        (t + 1, r),
                    ).start()
            else:
                remote(
                    block, block, line_send.at[slot, 1],
                    line_recv.at[slot, v, c], (t, spot * 2 + 1 - lane),
                ).start()

        for c in range(chunks):
            if isinstance(d, int):
                for w in range(2):
                    for k in range(picks):
                        i = pick(r, w, k)
                        v = place_of(r, i)
                        which = w * picks + k

                        @pl.when(i < per)
                        def _():
                            unit_chunk(j, v, c).wait_recv()
                            forward(0, c, v, which)
                            forward(1, c, v, which)
                            aside(0, c, v, which)
            else:
                def act(stream, ok, v, which):
                    @pl.when(ok)
                    def _():
                        unit_chunk(j, v, c).wait_recv()
                        forward(stream, c, v, which)
                        aside(stream, c, v, which)

                line_units(d, act)

    def unit_chunk(j, v, c):
        block = e_half.at[j, unit_span(v, c, CHUNK), :]
        return remote(
            block, block, init_send.at[0], line_recv.at[slot_of(j), v, c], (partner, r)
        )

    def line_gone(j, with_pass):
        slot = slot_of(j)
        along = [
            sum([1 - (plane_of(at * 2 + lane, i) + p) % 2 for i in range(per)])
            for at in range(spots)
        ]
        beside = sum(along)
        ahead = 0
        for at in range(spots):
            ahead = ahead + along[at] * jnp.where((at <= spot) & (spot < spots - 1), 1, 0)
            ahead = ahead + along[at] * jnp.where((at >= spot) & (spot > 0), 1, 0)

        def sent(count, total, sem):
            @pl.when(count == total)
            def _():
                block = e_half.at[j, pl.ds(0, total * unit), :]
                remote(block, block, sem, line_recv.at[0, 0, 0], (partner, r)).wait_send()

        for total in line_totals(rows, n)[0]:
            sent(beside, total, line_send.at[slot, 1])
            if with_pass:
                sent(beside, total, pass_send.at[slot])
        for total in line_totals(rows, n)[1]:
            sent(ahead, total, line_send.at[slot, 0])

    def l_copy(j, plane, tile):
        return remote(
            cov_hbm.at[:, nat_columns(tile, plane)],
            l_in.at[j, :, half_columns(tile)],
            l_send.at[plane], l_recv.at[j], (b + 2 * plane + 1, r),
        )

    def l_local(j, tile):
        return pltpu.make_async_copy(
            cov_hbm.at[:, nat_columns(tile, p)], l_in.at[j, :, half_columns(tile)],
            l_recv.at[j],
        )

    def l_whole(j, plane):
        return remote(
            l_in.at[j], l_in.at[j], l_send.at[plane], l_recv.at[j], (partner, r)
        )

    def top_copy():
        return remote(
            cov_hbm, cov.at[3, pl.ds(0, rows), :], top_sems.at[0], top_sems.at[1], (t - 2 * (2 * p - 1), r)
        )

    def g_copy(plane):
        return remote(
            offset_in, gbuf.at[r, j_own], g_send.at[plane], g_recv.at[0], (b + 2 * plane + 1, r)
        )

    def g_bundle(o, source):
        return remote(gbuf.at[source], gbuf.at[source], gb_send.at[0], gb_recv.at[0], (t, o))

    def left_copy(j, d, i, v):
        return remote(
            left_out.at[j, v], left_in.at[j, r, i], left_send.at[j], left_recv.at[j % 2, r], (t, d)
        )

    def left_across(j, v, i):
        return remote(
            left_out.at[j, v], left_in.at[j, r, i], left_send.at[j], across_recv.at[j % 2, r],
            (partner, r),
        )

    def left_block(j, o, start, count, recv):
        block = left_in.at[j, o, pl.ds(start, count)]
        return remote(block, block, fwd_send.at[j], recv, (partner, r))

    def left_sent(j):
        remote(
            left_out.at[j], left_out.at[j], left_send.at[j], left_recv.at[j % 2, r], (partner, r)
        ).wait_send()

    def left_pass(j, o, count):
        return left_block(j, o, first_held, count, across_recv.at[j % 2, o])

    def pass_sent(j, count):
        block = left_in.at[j, pl.ds(0, n - 1), pl.ds(0, count)]
        remote(block, block, fwd_send.at[j], across_recv.at[j % 2, r], (partner, r)).wait_send()

    def x_copy(j, tile, plane):
        columns = nat_columns(tile, plane)
        return remote(
            cov.at[j, :, columns], cov.at[j, :, columns], x_send.at[j], x_recv.at[j],
            (partner, r),
        )

    def x_whole(j):
        block = cov.at[j, :, pl.ds(0, half)]
        return remote(block, block, x_send.at[j], x_recv.at[j], (partner, r))

    def out_copy(tile, plane):
        columns = nat_columns(tile, plane)
        return remote(
            cov.at[0, :, columns], out.at[:, columns], out_sems.at[0], out_sems.at[1], (b, r),
        )

    def out_arrival():
        return remote(cov.at[0], out, out_sems.at[0], out_sems.at[1], (t + 1, r))

    def out_gone():
        block = cov.at[0, :, pl.ds(0, half)]
        remote(block, out.at[:, pl.ds(0, half)], out_sems.at[0], out_sems.at[1], (b, r)).wait_send()

    def mid_copy():
        return remote(cov.at[2], out, mid_sems.at[0], mid_sems.at[1], (b + 2, r))

    def low_copy(tile, plane, dest):
        columns = nat_columns(tile, plane)
        return remote(
            cov.at[0, :, columns], cov.at[gathers, :, columns], low_send.at[dest],
            low_recv.at[0], (b - 4 + 2 * dest + 1, r),
        )

    def both(copies, what):
        for copy in copies:
            getattr(copy, what)()

    def send_l(j):
        for plane in range(2):
            for tile in range(tiles):
                @pl.when(b + 2 * plane + 1 != t)
                def _():
                    l_copy(j, plane, tile).start()

                @pl.when(b + 2 * plane + 1 == t)
                def _():
                    l_local(j, tile).start()

    def l_gone(j):
        for plane in range(2):
            @pl.when(b + 2 * plane + 1 != t)
            def _():
                l_whole(j, plane).wait_send()

    def send_g():
        for plane in range(2):
            @pl.when(b + 2 * plane + 1 != t)
            def _():
                g_copy(plane).start()

    def g_gone():
        for plane in range(2):
            @pl.when(b + 2 * plane + 1 != t)
            def _():
                g_copy(plane).wait_send()

    @pl.when(core == 0)
    def _mover():
        @pl.when(j_own == 2)
        def _():
            source(2, "start")
            send_g()

        @pl.when(j_own == 0)
        def _():
            send_g()
            source(0, "start")
            send_l(0)

        if quads > 1:
            @pl.when(q < quads - 1)
            def _():
                line_hop(3, 0, True)

                def hop3(d, carry):
                    line_hop(3, d, True)
                    return carry

                lax.fori_loop(1, spots, hop3, 0)

        line_hop(1, 0, True)

        def hop_step(d, carry):
            @pl.when(d == SPREAD_AT)
            def _():
                @pl.when(j_own == 2)
                def _():
                    send_l(2)

            @pl.when(d < spots)
            def _():
                line_hop(1, d, True)

            @pl.when(d == BEHIND)
            def _():
                line_hop(0, 0, True)

            @pl.when(d > BEHIND)
            def _():
                line_hop(0, d - BEHIND, True)

            return carry

        lax.fori_loop(1, spots + BEHIND, hop_step, 0)

        if quads > 1:
            @pl.when(q < quads - 1)
            def _():
                line_gone(3, True)

        line_gone(1, True)
        line_gone(0, True)

        @pl.when(j_own == 2)
        def _():
            source_gone(2)
            l_gone(2)

        @pl.when(j_own == 0)
        def _():
            source_gone(0)
            l_gone(0)

        g_gone()

        @pl.when(j_own == 2)
        def _():
            mid_copy().wait_recv()

        @pl.when(j_own == 0)
        def _():
            out_arrival().wait_recv()

    @pl.when(core == 1)
    def _worker():
        send_g()

        pltpu.make_async_copy(offset_in, gbuf.at[r, j_own], g_recv.at[1]).start()

        def store_left(j, v, block):
            if rows == 192:
                left_out[j, v, 0:unit, :] = block[:, :LANES]
                for s in range(2):
                    left_out[j, v, unit:, s * 64:(s + 1) * 64] = block[
                        s * unit // 2:(s + 1) * unit // 2, LANES:
                    ]
            else:
                left_out[j, v] = block

        def place_left(j, d, i):
            at, low = d * rows, i * unit
            if rows == 192:
                left[low:low + unit, at:at + LANES] = left_in[j, d, i, 0:unit, :]
                for s in range(2):
                    left[low + s * unit // 2:low + (s + 1) * unit // 2, at + LANES:at + rows] = (
                        left_in[j, d, i, unit:, s * 64:(s + 1) * 64]
                    )
            else:
                left[low:low + unit, at:at + rows] = left_in[j, d, i]

        def send_left(j, v, d, i):
            @pl.when(d != r)
            def _():
                left_copy(j, d, i, v).start()

            @pl.when(d == r)
            def _():
                left_across(j, v, i).start()
                left_in[j, r, i] = left_out[j, v]

        def left_unit(o, i):
            v = place_of(o, i)
            product = lax.dot_general(
                e_half[2, unit_span(v, 0, unit), :], cov[3, 0:rows, :], CONTRACT_LAST,
                preferred_element_type=jnp.float32,
            )
            store_left(2, v, product.astype(jnp.bfloat16))
            send_left(2, v, o, i)

        def later(d):
            @pl.when((d == TOP_AT) & (j_own == 3) & top)
            def _():
                top_copy().start()

            @pl.when((d == 1) & (j_own == 1))
            def _():
                send_l(1)

            @pl.when(d == GAIN_AT)
            def _():
                @pl.when(j_own == 1)
                def _():
                    source(1, "start")

                if quads > 1:
                    @pl.when((j_own == 3) & jnp.logical_not(top))
                    def _():
                        source(3, "start")
                        send_l(3)

            @pl.when(d == BUNDLE_AT)
            def _():
                remote(
                    gbuf.at[r, pl.ds(0, 3)], gbuf.at[r, pl.ds(0, 3)], g_send.at[0], g_recv.at[0],
                    (partner, r),
                ).wait_recv()

        line_hop(2, 0, False)

        def e2_hop(d, carry):
            line_hop(2, d, False)
            later(d)
            return carry

        lax.fori_loop(1, spots, e2_hop, 0)

        @pl.when(top)
        def _():
            @pl.when(j_own == 1)
            def _():
                top_copy().wait_recv()

            @pl.when(j_own == 3)
            def _():
                pltpu.make_async_copy(
                    cov_hbm, cov.at[3, pl.ds(0, rows), :], load_sems.at[0]
                ).wait()

            def own_lane(at, carry):
                for i in range(per):
                    @pl.when(plane_of(at * 2 + lane, i) == p)
                    def _():
                        left_unit(at * 2 + lane, i)
                return carry

            lax.fori_loop(0, spots, own_lane, 0)

        def other_lane(d, carry):
            for side in range(2):
                at = spot - d if side == 0 else spot + d
                o = at * 2 + 1 - lane
                for i in range(per):
                    @pl.when(
                        (at >= 0) & (at < spots) & ((side == 0) | (d > 0))
                        & (plane_of(o, i) == p)
                    )
                    def _():
                        for c in range(chunks):
                            unit_chunk(2, place_of(o, i), c).wait_recv()

                        @pl.when(top)
                        def _():
                            left_unit(o, i)
            return carry

        lax.fori_loop(0, spots, other_lane, 0)

        def bundles():
            return remote(
                gbuf.at[pl.ds(0, n - 1)], gbuf.at[pl.ds(0, n - 1)], gb_send.at[0], gb_recv.at[0],
                (partner, r),
            )

        pltpu.make_async_copy(offset_in, gbuf.at[r, j_own], g_recv.at[1]).wait()

        def bundle(i, c):
            g_bundle(other_row(i), r).start()
            return c

        lax.fori_loop(1, n, bundle, 0)

        first_step = jnp.where(top, 2, 3) if quads > 1 else 2
        started = jnp.where(top, 1, 0)

        def chain(k, carry):
            j = first_step - k

            if quads > 1:
                @pl.when(jnp.logical_not(top) & (j == 3))
                def _():
                    remote(
                        cov.at[0], cov.at[gathers], low_send.at[0], low_recv.at[0], (partner, r)
                    ).wait_recv()

            @pl.when(k >= started)
            def _():
                @pl.when(j != 2)
                def _():
                    whole_arrival(j).wait_recv()

                share = units // LEFT_PARTS

                def left_part(g, c):
                    span = pl.ds(aligned(g * share * unit, share * unit), share * unit)
                    product = lax.dot_general(
                        e_half[j, span, :], cov[j + 1, 0:rows, :], CONTRACT_LAST,
                        preferred_element_type=jnp.float32,
                    ).astype(jnp.bfloat16)
                    for i in range(share):
                        store_left(j, g * share + i, product[i * unit:(i + 1) * unit])

                    def send(i, cc):
                        v = g * share + i
                        d, at = owner(v)
                        send_left(j, v, d, at)
                        return cc

                    lax.fori_loop(0, share, send, 0)
                    return c

                lax.fori_loop(0, LEFT_PARTS, left_part, 0)

            for count in counts:
                @pl.when(held == count)
                def _():
                    def pass_on(i, c):
                        o = other_row(i)
                        left_block(j, o, first_held, count, left_recv.at[j % 2, o]).wait_recv()
                        left_pass(j, o, count).start()
                        return c

                    lax.fori_loop(1, n, pass_on, 0)

            for count in counts:
                @pl.when(per - held == count)
                def _():
                    def take(i, c):
                        left_block(j, i, first_other, count, across_recv.at[j % 2, i]).wait_recv()
                        return c

                    lax.fori_loop(0, n, take, 0)

            @pl.when(k == 0)
            def _():
                bundles().wait_recv()
                for i in range(n):
                    gsum[:, :, i * rows:(i + 1) * rows] = gbuf[i].astype(jnp.float32)

                @pl.when(top)
                def _():
                    cov[3, rows:, :] = jnp.broadcast_to(gsum[3], (PAD, size)).astype(jnp.bfloat16)

            for d in range(n):
                for at in range(per):
                    place_left(j, d, at)
            left[rows:, :] = cov[j + 1, rows:, :]

            l_whole(j, 0).wait_recv()

            def right_part(g, c):
                wide = TILES_AT_ONCE * LANES
                product = lax.dot_general(
                    left[...], e_half[j, pl.ds(aligned(g * wide, wide), wide), :], CONTRACT_LAST,
                    preferred_element_type=jnp.float32,
                )
                for s in range(TILES_AT_ONCE):
                    tile = g * TILES_AT_ONCE + s
                    columns = nat_columns(tile, p)
                    block = product[:, s * LANES:(s + 1) * LANES]
                    cov[j, 0:rows, columns] = (
                        block[:rows] + l_in[j, :, half_columns(tile)].astype(jnp.float32)
                    ).astype(jnp.bfloat16)
                    cov[j, rows:, columns] = (
                        block[rows:] + gsum[j, :, columns]
                    ).astype(jnp.bfloat16)

                    @pl.when(j > 0)
                    def _():
                        x_copy(j, tile, p).start()

                    @pl.when(j == 0)
                    def _():
                        out_copy(tile, p).start()
                        if quads > 1:
                            @pl.when(q > 0)
                            def _():
                                for dest in range(2):
                                    low_copy(tile, p, dest).start()
                return c

            lax.fori_loop(0, tiles // TILES_AT_ONCE, right_part, 0)

            @pl.when(j > 0)
            def _():
                x_whole(j).wait_recv()

            @pl.when((j == 2) & (j_own == 3))
            def _():
                mid_copy().start()

            return carry

        lax.fori_loop(0, first_step + 1, chain, 0)

        out[...] = cov[j_own]

        def sent(k, carry):
            j = first_step - k

            left_sent(j)
            for count in counts:
                @pl.when(held == count)
                def _():
                    pass_sent(j, count)

            @pl.when(j > 0)
            def _():
                x_whole(j).wait_send()

            return carry

        lax.fori_loop(0, first_step + 1, sent, 0)

        line_gone(2, False)
        bundles().wait_send()
        out_gone()
        if quads > 1:
            @pl.when(q > 0)
            def _():
                for dest in range(2):
                    remote(
                        cov.at[0, :, pl.ds(0, half)], cov.at[gathers, :, pl.ds(0, half)],
                        low_send.at[dest], low_recv.at[0], (partner, r),
                    ).wait_send()
        g_gone()

        @pl.when(j_own == 1)
        def _():
            source_gone(1)
            l_gone(1)

        if quads > 1:
            @pl.when((j_own == 3) & jnp.logical_not(top))
            def _():
                source_gone(3)
                l_gone(3)

        @pl.when((j_own == 3) & top)
        def _():
            top_copy().wait_send()

        @pl.when(j_own == 3)
        def _():
            mid_copy().wait_send()


def shards(steps, n, smoother_gains, smoother_offsets, smoother_covs):
    own_gain = smoother_gains[0]
    own_cov = smoother_covs[0]
    rows, size = own_cov.shape
    start = lax.axis_index("rows") * rows
    vmem = pl.BlockSpec(memory_space=pltpu.VMEM)
    hbm = pl.BlockSpec(memory_space=pltpu.HBM)
    gathers = 3 if steps == 4 else 4
    half = size // 2
    unit = unit_rows(rows)
    per = rows // unit
    chunks = unit // CHUNK
    tiles = half // LANES
    units = half // unit
    upt = LANES // unit
    slots = 2 if steps == 4 else 3
    bf16 = jnp.bfloat16
    dma = pltpu.SemaphoreType.DMA
    both = pl.pallas_call(
        functools.partial(kernel, steps, n),
        out_shape=jax.ShapeDtypeStruct((rows + PAD, size), bf16),
        in_specs=[hbm, hbm, hbm],
        out_specs=vmem,
        scratch_shapes=[
            pltpu.VMEM((gathers, half, size), bf16),
            pltpu.VMEM((gathers + 1, rows + PAD, size), bf16),
            pltpu.VMEM((gathers, rows, half), bf16),
            pltpu.VMEM((gathers, units) + folded(rows), bf16),
            pltpu.VMEM((gathers, n, per) + folded(rows), bf16),
            pltpu.VMEM((rows + PAD, size), bf16),
            pltpu.VMEM((n, 4, 1, rows), bf16),
            pltpu.VMEM((4, 1, size), jnp.float32),
            dma((slots, 2)),
            dma((slots, units, chunks)),
            dma((slots,)),
            dma((gathers,)),
            dma((1,)),
            dma((2,)),
            dma((gathers,)),
            dma((2,)),
            dma((1,)),
            dma((2,)),
            dma((2,)),
            dma((1,)),
            dma((1,)),
            dma((gathers,)),
            dma((2, n)),
            dma((2, n)),
            dma((gathers,)),
            dma((gathers,)),
            dma((gathers,)),
            dma((2,)),
            dma((2,)),
            dma((2,)),
            dma((1,)),
        ],
        compiler_params=pltpu.CompilerParams(
            collective_id=0, has_side_effects=True, vmem_limit_bytes=40 << 20
        ),
    )(pltpu.with_memory_space_constraint(own_gain, pltpu.HBM), pltpu.with_memory_space_constraint(smoother_offsets, pltpu.HBM), pltpu.with_memory_space_constraint(own_cov, pltpu.HBM))
    mean = lax.dynamic_slice(both, (rows, start), (1, rows))
    return mean, both[None, :rows]


def solution(mesh):
    in_specs = (P("tm", "rows", None), P("tm", "rows"), P("tm", "rows", None))
    out_specs = (P("tm", "rows"), P("tm", "rows", None))
    body = functools.partial(shards, mesh.shape["tm"], mesh.shape["rows"])
    return jax.shard_map(body, mesh=mesh, in_specs=in_specs, out_specs=out_specs, check_vma=False)
```

```python
import functools
import math

import jax
import jax.numpy as jnp
from jax import lax
from jax.experimental import pallas as pl
from jax.experimental.pallas import tpu as pltpu
from jax.sharding import PartitionSpec as P

MESH = pl.DeviceIdType.MESH
LANES = 128
PAD = 16
CHUNK = 32
GAIN_AT = 2
TOP_AT = 1
BUNDLE_AT = 3
BEHIND = 3
SPREAD_AT = 1
LEFT_PARTS = 2
TILES_AT_ONCE = 1
CONTRACT_LAST = (((1,), (1,)), ((), ()))


def unit_rows(rows):
    return math.gcd(rows, LANES)


def share_sizes(rows, n):
    unit = unit_rows(rows)
    per, upt = rows // unit, LANES // unit
    planes = [[(per * d + i) // upt % 2 for i in range(per)] for d in range(n)]
    return sorted({row.count(x) for row in planes for x in range(2)})


def line_totals(rows, n):
    unit = unit_rows(rows)
    per, upt, spots = rows // unit, LANES // unit, n // 2
    beside, ahead = set(), set()
    for x in range(2):
        for lane in range(2):
            along = [
                sum((per * (at * 2 + lane) + i) // upt % 2 == x for i in range(per))
                for at in range(spots)
            ]
            beside.add(sum(along))
            for spot in range(spots):
                ahead.add(
                    (sum(along[:spot + 1]) if spot < spots - 1 else 0)
                    + (sum(along[spot:]) if spot > 0 else 0)
                )
    return sorted(beside), sorted(ahead)


def folded(rows):
    unit = unit_rows(rows)
    return (unit + unit // 2, LANES) if rows == 192 else (unit, rows)


def kernel(
    steps, n, gain_in, offset_in, cov_hbm, out,
    e_half, cov, l_in, left_out, left_in, left, gbuf, gsum,
    line_send, line_recv, pass_send, full_recv, init_send,
    l_send, l_recv, top_sems, load_sems, g_send, g_recv, gb_send, gb_recv,
    left_send, left_recv, across_recv, fwd_send, x_send, x_recv, out_sems, mid_sems,
    low_send, low_recv,
):
    t = lax.axis_index("tm")
    r = lax.axis_index("rows")
    spot, lane, spots = r // 2, r % 2, n // 2
    quads = steps // 4
    gathers = e_half.shape[0]
    q = t // 4
    b = q * 4
    j_own = t % 4
    p = j_own // 2
    core = t % 2
    top = q == quads - 1
    partner = b + 2 * (1 - p) + 1
    size = gain_in.shape[1]
    rows = size // n
    half = size // 2
    unit = unit_rows(rows)
    per = rows // unit
    upt = LANES // unit
    tiles = half // LANES
    units = half // unit
    chunks = unit // CHUNK
    picks = upt // 2
    sizes = share_sizes(rows, n)
    counts = [size for size in sizes if size]
    greet_all = 0 in sizes

    def aligned(x, m):
        return pl.multiple_of(x, m)

    def remote(src, dst, send, recv, device):
        return pltpu.make_async_remote_copy(
            src_ref=src, dst_ref=dst, send_sem=send, recv_sem=recv,
            device_id=device, device_id_type=MESH,
        )

    def plane_of(d, i):
        return ((per * d + i) // upt) % 2

    def place_of(d, i):
        u = per * d + i
        return (u // upt // 2) * upt + u % upt

    def pick(o, w, k):
        start = per * o
        i = (upt * p + 2 * k + w - start + 2 * upt * n) % (2 * upt)
        return i

    mine = [plane_of(r, i) for i in range(per)]
    held = sum([1 - (x + p) % 2 for x in mine])
    first_held = (1 - (mine[0] + p) % 2) * 0 + ((mine[0] + p) % 2) * (per - held)
    first_other = (1 - (mine[0] + p) % 2) * held

    def owner(v):
        u = ((v // upt) * 2 + p) * upt + v % upt
        return u // per, u % per

    def unit_span(v, c, length):
        return pl.ds(aligned(v * unit + c * CHUNK, CHUNK), length)

    def nat_columns(tile, plane):
        return pl.ds(aligned((tile * 2 + plane) * LANES, LANES), LANES)

    def half_columns(tile):
        return pl.ds(aligned(tile * LANES, LANES), LANES)

    def other_row(i):
        return (r + i) % n

    barrier = pltpu.get_barrier_semaphore()

    def greet(tt, rr):
        pl.semaphore_signal(barrier, inc=1, device_id=(tt, rr), device_id_type=MESH)

    for i in range(1, 4):
        greet(b + (j_own + i) % 4, r)
    greet(t, spot * 2 + 1 - lane)
    greet(t + 1 - 2 * core, spot * 2 + 1 - lane)

    @pl.when(spot > 0)
    def _():
        greet(t, r - 2)

    @pl.when(spot < spots - 1)
    def _():
        greet(t, r + 2)

    inner = (spot + spots - 1) // spots + (2 * spots - 2 - spot) // spots
    greetings = 5 + inner
    if greet_all:
        @pl.when(core == 1)
        def _():
            def greet_row(i, carry):
                o = other_row(i)
                near = (o // 2 == spot) | ((o % 2 == lane) & (o // 2 - spot < 2) & (spot - o // 2 < 2))

                @pl.when(jnp.logical_not(near))
                def _():
                    greet(t, o)
                return carry

            lax.fori_loop(1, n, greet_row, 0)

        greetings = greetings + core * (n - 2 - inner)
    if quads > 1:
        for step in (-4, 4):
            near = (q * 4 + step >= 0) & (q * 4 + step < steps)

            @pl.when((core == 1) & near)
            def _():
                for i in (1, 3):
                    greet(b + step + i, r)

        greetings = greetings + core * 2 * (((q + quads - 1) // quads) + (2 * quads - 2 - q) // quads * 1)

    @pl.when(j_own == 3)
    def _():
        pltpu.make_async_copy(cov_hbm, cov.at[3, pl.ds(0, rows), :], load_sems.at[0]).start()

    pl.semaphore_wait(barrier, greetings)

    def slot_of(j):
        return 0 if j == 2 else (2 if j == 3 else j)

    def source(j, what):
        for i in range(per):
            x, v = plane_of(r, i), place_of(r, i)
            to = b + 2 * x + (1 if j == 2 else 0)
            for c in range(chunks):
                src = gain_in.at[pl.ds(i * unit + c * CHUNK, CHUNK), :]
                dst = e_half.at[j, unit_span(v, c, CHUNK), :]
                recv = line_recv.at[slot_of(j), v, c]

                def go():
                    remote(src, dst, init_send.at[0], recv, (to, r)).start()

                if j == 0:
                    @pl.when(to == t)
                    def _():
                        pltpu.make_async_copy(src, dst, recv).start()

                    pl.when(to != t)(go)
                else:
                    go()

    def source_gone(j):
        for count in ([per] if j else counts + [0]):
            @pl.when((per - held == count) | (j != 0))
            def _():
                if count:
                    block = gain_in.at[pl.ds(0, count * unit), :]
                    remote(
                        block, e_half.at[j, pl.ds(0, count * unit), :], init_send.at[0],
                        line_recv.at[0, 0, 0], (partner, r),
                    ).wait_send()

    def whole_arrival(j):
        return remote(e_half.at[j], e_half.at[j], init_send.at[0], full_recv.at[j], (t - 1, r))

    def unit_of(j, v):
        return e_half.at[j, unit_span(v, 0, unit), :]

    def line_units(d, act):
        for stream in range(2):
            at = spot - d if stream == 0 else spot + d
            inside = (at >= 0) & (at < spots)
            o = jnp.where(inside, at * 2 + lane, r)
            for w in range(2):
                for k in range(picks):
                    i = pick(o, w, k)
                    act(stream, inside & (i < per), place_of(o, i), w * picks + k)

    def onward(stream):
        return (spot < spots - 1) if stream == 0 else (spot > 0)

    def line_hop(j, d, with_pass):
        slot = slot_of(j)

        def forward(stream, c, v, which):
            span = unit_span(v, c, CHUNK)
            block = e_half.at[j, span, :]

            @pl.when(onward(stream))
            def _():
                remote(
                    block, block, line_send.at[slot, 0],
                    line_recv.at[slot, v, c], (t, r + 2 if stream == 0 else r - 2),
                ).start()

        def aside(stream, c, v, which):
            block = e_half.at[j, unit_span(v, c, CHUNK), :]
            if with_pass:
                remote(
                    block, block, line_send.at[slot, 1], full_recv.at[j],
                    (t + 1, spot * 2 + 1 - lane),
                ).start()
                if c == chunks - 1:
                    block = unit_of(j, v)
                    remote(
                        block, block, pass_send.at[slot], full_recv.at[j],
                        (t + 1, r),
                    ).start()
            else:
                remote(
                    block, block, line_send.at[slot, 1],
                    line_recv.at[slot, v, c], (t, spot * 2 + 1 - lane),
                ).start()

        for c in range(chunks):
            if isinstance(d, int):
                for w in range(2):
                    for k in range(picks):
                        i = pick(r, w, k)
                        v = place_of(r, i)
                        which = w * picks + k

                        @pl.when(i < per)
                        def _():
                            unit_chunk(j, v, c).wait_recv()
                            forward(0, c, v, which)
                            forward(1, c, v, which)
                            aside(0, c, v, which)
            else:
                def act(stream, ok, v, which):
                    @pl.when(ok)
                    def _():
                        unit_chunk(j, v, c).wait_recv()
                        forward(stream, c, v, which)
                        aside(stream, c, v, which)

                line_units(d, act)

    def unit_chunk(j, v, c):
        block = e_half.at[j, unit_span(v, c, CHUNK), :]
        return remote(
            block, block, init_send.at[0], line_recv.at[slot_of(j), v, c], (partner, r)
        )

    def line_gone(j, with_pass):
        slot = slot_of(j)
        along = [
            sum([1 - (plane_of(at * 2 + lane, i) + p) % 2 for i in range(per)])
            for at in range(spots)
        ]
        beside = sum(along)
        ahead = 0
        for at in range(spots):
            ahead = ahead + along[at] * jnp.where((at <= spot) & (spot < spots - 1), 1, 0)
            ahead = ahead + along[at] * jnp.where((at >= spot) & (spot > 0), 1, 0)

        def sent(count, total, sem):
            @pl.when(count == total)
            def _():
                block = e_half.at[j, pl.ds(0, total * unit), :]
                remote(block, block, sem, line_recv.at[0, 0, 0], (partner, r)).wait_send()

        for total in line_totals(rows, n)[0]:
            sent(beside, total, line_send.at[slot, 1])
            if with_pass:
                sent(beside, total, pass_send.at[slot])
        for total in line_totals(rows, n)[1]:
            sent(ahead, total, line_send.at[slot, 0])

    def l_copy(j, plane, tile):
        return remote(
            cov_hbm.at[:, nat_columns(tile, plane)],
            l_in.at[j, :, half_columns(tile)],
            l_send.at[plane], l_recv.at[j], (b + 2 * plane + 1, r),
        )

    def l_local(j, tile):
        return pltpu.make_async_copy(
            cov_hbm.at[:, nat_columns(tile, p)], l_in.at[j, :, half_columns(tile)],
            l_recv.at[j],
        )

    def l_whole(j, plane):
        return remote(
            l_in.at[j], l_in.at[j], l_send.at[plane], l_recv.at[j], (partner, r)
        )

    def top_copy():
        return remote(
            cov_hbm, cov.at[3, pl.ds(0, rows), :], top_sems.at[0], top_sems.at[1], (t - 2 * (2 * p - 1), r)
        )

    def g_copy(plane):
        return remote(
            offset_in, gbuf.at[r, j_own], g_send.at[plane], g_recv.at[0], (b + 2 * plane + 1, r)
        )

    def g_bundle(o, source):
        return remote(gbuf.at[source], gbuf.at[source], gb_send.at[0], gb_recv.at[0], (t, o))

    def left_copy(j, d, i, v):
        return remote(
            left_out.at[j, v], left_in.at[j, r, i], left_send.at[j], left_recv.at[j % 2, r], (t, d)
        )

    def left_across(j, v, i):
        return remote(
            left_out.at[j, v], left_in.at[j, r, i], left_send.at[j], across_recv.at[j % 2, r],
            (partner, r),
        )

    def left_block(j, o, start, count, recv):
        block = left_in.at[j, o, pl.ds(start, count)]
        return remote(block, block, fwd_send.at[j], recv, (partner, r))

    def left_sent(j):
        remote(
            left_out.at[j], left_out.at[j], left_send.at[j], left_recv.at[j % 2, r], (partner, r)
        ).wait_send()

    def left_pass(j, o, count):
        return left_block(j, o, first_held, count, across_recv.at[j % 2, o])

    def pass_sent(j, count):
        block = left_in.at[j, pl.ds(0, n - 1), pl.ds(0, count)]
        remote(block, block, fwd_send.at[j], across_recv.at[j % 2, r], (partner, r)).wait_send()

    def x_copy(j, tile, plane):
        columns = nat_columns(tile, plane)
        return remote(
            cov.at[j, :, columns], cov.at[j, :, columns], x_send.at[j], x_recv.at[j],
            (partner, r),
        )

    def x_whole(j):
        block = cov.at[j, :, pl.ds(0, half)]
        return remote(block, block, x_send.at[j], x_recv.at[j], (partner, r))

    def out_copy(tile, plane):
        columns = nat_columns(tile, plane)
        return remote(
            cov.at[0, :, columns], out.at[:, columns], out_sems.at[0], out_sems.at[1], (b, r),
        )

    def out_arrival():
        return remote(cov.at[0], out, out_sems.at[0], out_sems.at[1], (t + 1, r))

    def out_gone():
        block = cov.at[0, :, pl.ds(0, half)]
        remote(block, out.at[:, pl.ds(0, half)], out_sems.at[0], out_sems.at[1], (b, r)).wait_send()

    def mid_copy():
        return remote(cov.at[2], out, mid_sems.at[0], mid_sems.at[1], (b + 2, r))

    def low_copy(tile, plane, dest):
        columns = nat_columns(tile, plane)
        return remote(
            cov.at[0, :, columns], cov.at[gathers, :, columns], low_send.at[dest],
            low_recv.at[0], (b - 4 + 2 * dest + 1, r),
        )

    def both(copies, what):
        for copy in copies:
            getattr(copy, what)()

    def send_l(j):
        for plane in range(2):
            for tile in range(tiles):
                @pl.when(b + 2 * plane + 1 != t)
                def _():
                    l_copy(j, plane, tile).start()

                @pl.when(b + 2 * plane + 1 == t)
                def _():
                    l_local(j, tile).start()

    def l_gone(j):
        for plane in range(2):
            @pl.when(b + 2 * plane + 1 != t)
            def _():
                l_whole(j, plane).wait_send()

    def send_g():
        for plane in range(2):
            @pl.when(b + 2 * plane + 1 != t)
            def _():
                g_copy(plane).start()

    def g_gone():
        for plane in range(2):
            @pl.when(b + 2 * plane + 1 != t)
            def _():
                g_copy(plane).wait_send()

    @pl.when(core == 0)
    def _mover():
        @pl.when(j_own == 2)
        def _():
            source(2, "start")
            send_g()

        @pl.when(j_own == 0)
        def _():
            send_g()
            source(0, "start")
            send_l(0)

        if quads > 1:
            @pl.when(q < quads - 1)
            def _():
                line_hop(3, 0, True)

                def hop3(d, carry):
                    line_hop(3, d, True)
                    return carry

                lax.fori_loop(1, spots, hop3, 0)

        line_hop(1, 0, True)

        def hop_step(d, carry):
            @pl.when(d == SPREAD_AT)
            def _():
                @pl.when(j_own == 2)
                def _():
                    send_l(2)

            @pl.when(d < spots)
            def _():
                line_hop(1, d, True)

            @pl.when(d == BEHIND)
            def _():
                line_hop(0, 0, True)

            @pl.when(d > BEHIND)
            def _():
                line_hop(0, d - BEHIND, True)

            return carry

        lax.fori_loop(1, spots + BEHIND, hop_step, 0)

        if quads > 1:
            @pl.when(q < quads - 1)
            def _():
                line_gone(3, True)

        line_gone(1, True)
        line_gone(0, True)

        @pl.when(j_own == 2)
        def _():
            source_gone(2)
            l_gone(2)

        @pl.when(j_own == 0)
        def _():
            source_gone(0)
            l_gone(0)

        g_gone()

        @pl.when(j_own == 2)
        def _():
            mid_copy().wait_recv()

        @pl.when(j_own == 0)
        def _():
            out_arrival().wait_recv()

    @pl.when(core == 1)
    def _worker():
        send_g()

        pltpu.make_async_copy(offset_in, gbuf.at[r, j_own], g_recv.at[1]).start()

        def store_left(j, v, block):
            if rows == 192:
                left_out[j, v, 0:unit, :] = block[:, :LANES]
                for s in range(2):
                    left_out[j, v, unit:, s * 64:(s + 1) * 64] = block[
                        s * unit // 2:(s + 1) * unit // 2, LANES:
                    ]
            else:
                left_out[j, v] = block

        def place_left(j, d, i):
            at, low = d * rows, i * unit
            if rows == 192:
                left[low:low + unit, at:at + LANES] = left_in[j, d, i, 0:unit, :]
                for s in range(2):
                    left[low + s * unit // 2:low + (s + 1) * unit // 2, at + LANES:at + rows] = (
                        left_in[j, d, i, unit:, s * 64:(s + 1) * 64]
                    )
            else:
                left[low:low + unit, at:at + rows] = left_in[j, d, i]

        def send_left(j, v, d, i):
            @pl.when(d != r)
            def _():
                left_copy(j, d, i, v).start()

            @pl.when(d == r)
            def _():
                left_across(j, v, i).start()
                left_in[j, r, i] = left_out[j, v]

        def left_unit(o, i):
            v = place_of(o, i)
            product = lax.dot_general(
                e_half[2, unit_span(v, 0, unit), :], cov[3, 0:rows, :], CONTRACT_LAST,
                preferred_element_type=jnp.float32,
            )
            store_left(2, v, product.astype(jnp.bfloat16))
            send_left(2, v, o, i)

        def later(d):
            @pl.when((d == TOP_AT) & (j_own == 3) & top)
            def _():
                top_copy().start()

            @pl.when((d == 1) & (j_own == 1))
            def _():
                send_l(1)

            @pl.when(d == GAIN_AT)
            def _():
                @pl.when(j_own == 1)
                def _():
                    source(1, "start")

                if quads > 1:
                    @pl.when((j_own == 3) & jnp.logical_not(top))
                    def _():
                        source(3, "start")
                        send_l(3)

            @pl.when(d == BUNDLE_AT)
            def _():
                remote(
                    gbuf.at[r, pl.ds(0, 3)], gbuf.at[r, pl.ds(0, 3)], g_send.at[0], g_recv.at[0],
                    (partner, r),
                ).wait_recv()

        line_hop(2, 0, False)

        def e2_hop(d, carry):
            line_hop(2, d, False)
            later(d)
            return carry

        lax.fori_loop(1, spots, e2_hop, 0)

        @pl.when(top)
        def _():
            @pl.when(j_own == 1)
            def _():
                top_copy().wait_recv()

            @pl.when(j_own == 3)
            def _():
                pltpu.make_async_copy(
                    cov_hbm, cov.at[3, pl.ds(0, rows), :], load_sems.at[0]
                ).wait()

            def own_lane(at, carry):
                for i in range(per):
                    @pl.when(plane_of(at * 2 + lane, i) == p)
                    def _():
                        left_unit(at * 2 + lane, i)
                return carry

            lax.fori_loop(0, spots, own_lane, 0)

        def other_lane(d, carry):
            for side in range(2):
                at = spot - d if side == 0 else spot + d
                o = at * 2 + 1 - lane
                for i in range(per):
                    @pl.when(
                        (at >= 0) & (at < spots) & ((side == 0) | (d > 0))
                        & (plane_of(o, i) == p)
                    )
                    def _():
                        for c in range(chunks):
                            unit_chunk(2, place_of(o, i), c).wait_recv()

                        @pl.when(top)
                        def _():
                            left_unit(o, i)
            return carry

        lax.fori_loop(0, spots, other_lane, 0)

        def bundles():
            return remote(
                gbuf.at[pl.ds(0, n - 1)], gbuf.at[pl.ds(0, n - 1)], gb_send.at[0], gb_recv.at[0],
                (partner, r),
            )

        pltpu.make_async_copy(offset_in, gbuf.at[r, j_own], g_recv.at[1]).wait()

        def bundle(i, c):
            g_bundle(other_row(i), r).start()
            return c

        lax.fori_loop(1, n, bundle, 0)

        first_step = jnp.where(top, 2, 3) if quads > 1 else 2
        started = jnp.where(top, 1, 0)

        def chain(k, carry):
            j = first_step - k

            if quads > 1:
                @pl.when(jnp.logical_not(top) & (j == 3))
                def _():
                    remote(
                        cov.at[0], cov.at[gathers], low_send.at[0], low_recv.at[0], (partner, r)
                    ).wait_recv()

            @pl.when(k >= started)
            def _():
                @pl.when(j != 2)
                def _():
                    whole_arrival(j).wait_recv()

                share = units // LEFT_PARTS

                def left_part(g, c):
                    span = pl.ds(aligned(g * share * unit, share * unit), share * unit)
                    product = lax.dot_general(
                        e_half[j, span, :], cov[j + 1, 0:rows, :], CONTRACT_LAST,
                        preferred_element_type=jnp.float32,
                    ).astype(jnp.bfloat16)
                    for i in range(share):
                        store_left(j, g * share + i, product[i * unit:(i + 1) * unit])

                    def send(i, cc):
                        v = g * share + i
                        d, at = owner(v)
                        send_left(j, v, d, at)
                        return cc

                    lax.fori_loop(0, share, send, 0)
                    return c

                lax.fori_loop(0, LEFT_PARTS, left_part, 0)

            for count in counts:
                @pl.when(held == count)
                def _():
                    def pass_on(i, c):
                        o = other_row(i)
                        left_block(j, o, first_held, count, left_recv.at[j % 2, o]).wait_recv()
                        left_pass(j, o, count).start()
                        return c

                    lax.fori_loop(1, n, pass_on, 0)

            for count in counts:
                @pl.when(per - held == count)
                def _():
                    def take(i, c):
                        left_block(j, i, first_other, count, across_recv.at[j % 2, i]).wait_recv()
                        return c

                    lax.fori_loop(0, n, take, 0)

            @pl.when(k == 0)
            def _():
                bundles().wait_recv()
                for i in range(n):
                    gsum[:, :, i * rows:(i + 1) * rows] = gbuf[i].astype(jnp.float32)

                @pl.when(top)
                def _():
                    cov[3, rows:, :] = jnp.broadcast_to(gsum[3], (PAD, size)).astype(jnp.bfloat16)

            for d in range(n):
                for at in range(per):
                    place_left(j, d, at)
            left[rows:, :] = cov[j + 1, rows:, :]

            l_whole(j, 0).wait_recv()

            def right_part(g, c):
                wide = TILES_AT_ONCE * LANES
                product = lax.dot_general(
                    left[...], e_half[j, pl.ds(aligned(g * wide, wide), wide), :], CONTRACT_LAST,
                    preferred_element_type=jnp.float32,
                )
                for s in range(TILES_AT_ONCE):
                    tile = g * TILES_AT_ONCE + s
                    columns = nat_columns(tile, p)
                    block = product[:, s * LANES:(s + 1) * LANES]
                    cov[j, 0:rows, columns] = (
                        block[:rows] + l_in[j, :, half_columns(tile)].astype(jnp.float32)
                    ).astype(jnp.bfloat16)
                    cov[j, rows:, columns] = (
                        block[rows:] + gsum[j, :, columns]
                    ).astype(jnp.bfloat16)

                    @pl.when(j > 0)
                    def _():
                        x_copy(j, tile, p).start()

                    @pl.when(j == 0)
                    def _():
                        out_copy(tile, p).start()
                        if quads > 1:
                            @pl.when(q > 0)
                            def _():
                                for dest in range(2):
                                    low_copy(tile, p, dest).start()
                return c

            lax.fori_loop(0, tiles // TILES_AT_ONCE, right_part, 0)

            @pl.when(j > 0)
            def _():
                x_whole(j).wait_recv()

            @pl.when((j == 2) & (j_own == 3))
            def _():
                mid_copy().start()

            return carry

        lax.fori_loop(0, first_step + 1, chain, 0)

        out[...] = cov[j_own]

        def sent(k, carry):
            j = first_step - k

            left_sent(j)
            for count in counts:
                @pl.when(held == count)
                def _():
                    pass_sent(j, count)

            @pl.when(j > 0)
            def _():
                x_whole(j).wait_send()

            return carry

        lax.fori_loop(0, first_step + 1, sent, 0)

        line_gone(2, False)
        bundles().wait_send()
        out_gone()
        if quads > 1:
            @pl.when(q > 0)
            def _():
                for dest in range(2):
                    remote(
                        cov.at[0, :, pl.ds(0, half)], cov.at[gathers, :, pl.ds(0, half)],
                        low_send.at[dest], low_recv.at[0], (partner, r),
                    ).wait_send()
        g_gone()

        @pl.when(j_own == 1)
        def _():
            source_gone(1)
            l_gone(1)

        if quads > 1:
            @pl.when((j_own == 3) & jnp.logical_not(top))
            def _():
                source_gone(3)
                l_gone(3)

        @pl.when((j_own == 3) & top)
        def _():
            top_copy().wait_send()

        @pl.when(j_own == 3)
        def _():
            mid_copy().wait_send()


def shards(steps, n, smoother_gains, smoother_offsets, smoother_covs):
    own_gain = smoother_gains[0]
    own_cov = smoother_covs[0]
    rows, size = own_cov.shape
    start = lax.axis_index("rows") * rows
    vmem = pl.BlockSpec(memory_space=pltpu.VMEM)
    hbm = pl.BlockSpec(memory_space=pltpu.HBM)
    gathers = 3 if steps == 4 else 4
    half = size // 2
    unit = unit_rows(rows)
    per = rows // unit
    chunks = unit // CHUNK
    tiles = half // LANES
    units = half // unit
    upt = LANES // unit
    slots = 2 if steps == 4 else 3
    bf16 = jnp.bfloat16
    dma = pltpu.SemaphoreType.DMA
    both = pl.pallas_call(
        functools.partial(kernel, steps, n),
        out_shape=jax.ShapeDtypeStruct((rows + PAD, size), bf16),
        in_specs=[hbm, hbm, hbm],
        out_specs=vmem,
        scratch_shapes=[
            pltpu.VMEM((gathers, half, size), bf16),
            pltpu.VMEM((gathers + 1, rows + PAD, size), bf16),
            pltpu.VMEM((gathers, rows, half), bf16),
            pltpu.VMEM((gathers, units) + folded(rows), bf16),
            pltpu.VMEM((gathers, n, per) + folded(rows), bf16),
            pltpu.VMEM((rows + PAD, size), bf16),
            pltpu.VMEM((n, 4, 1, rows), bf16),
            pltpu.VMEM((4, 1, size), jnp.float32),
            dma((slots, 2)),
            dma((slots, units, chunks)),
            dma((slots,)),
            dma((gathers,)),
            dma((1,)),
            dma((2,)),
            dma((gathers,)),
            dma((2,)),
            dma((1,)),
            dma((2,)),
            dma((2,)),
            dma((1,)),
            dma((1,)),
            dma((gathers,)),
            dma((2, n)),
            dma((2, n)),
            dma((gathers,)),
            dma((gathers,)),
            dma((gathers,)),
            dma((2,)),
            dma((2,)),
            dma((2,)),
            dma((1,)),
        ],
        compiler_params=pltpu.CompilerParams(
            collective_id=0, has_side_effects=True, vmem_limit_bytes=40 << 20
        ),
    )(pltpu.with_memory_space_constraint(own_gain, pltpu.HBM), pltpu.with_memory_space_constraint(smoother_offsets, pltpu.HBM), pltpu.with_memory_space_constraint(own_cov, pltpu.HBM))
    mean = lax.dynamic_slice(both, (rows, start), (1, rows))
    return mean, both[None, :rows]


def solution(mesh):
    in_specs = (P("tm", "rows", None), P("tm", "rows"), P("tm", "rows", None))
    out_specs = (P("tm", "rows"), P("tm", "rows", None))
    body = functools.partial(shards, mesh.shape["tm"], mesh.shape["rows"])
    return jax.shard_map(body, mesh=mesh, in_specs=in_specs, out_specs=out_specs, check_vma=False)
```
